32 devices in a mesh: seq: 4 (over y, core), batch: 8 (over z, x).
Axes of the slice: x: 2, y: 2, z: 4, core: 2. Of those that a mesh axis runs over, the one named last changes fastest.
Arguments:
- hidden: bfloat16 [32, 1024, 1472], P('batch', 'seq'), may hold values from -6 to 6
- keep_mask: int32 [32, 1024], P('batch'), may hold values from 0 to 1, as said below
- states_cotangent: bfloat16 [8, 4, 768, 1472], P('batch', 'seq'), may hold values from -6 to 6
- gate_cotangent: float32 [32, 1024], P('batch', 'seq'), may hold values from -6 to 6
- step_count: int32 [1], replicated, may hold values from 2 to 20
- attend_weight: float32 [1472, 1152], P(None, ('seq', 'batch')), may hold values from -0.0546875 to 0.0546875
- attend_first: float32 [1472, 1152], P(None, ('seq', 'batch'))
- attend_second: float32 [1472, 1152], P(None, ('seq', 'batch'))
- attend_average: float32 [1472, 1152], P(None, ('seq', 'batch')), may hold values from -0.0546875 to 0.0546875
- output_weight: float32 [384, 1472], P(('seq', 'batch')), may hold values from -12 to 12
- output_first: float32 [384, 1472], P(('seq', 'batch'))
- output_second: float32 [384, 1472], P(('seq', 'batch'))
- output_average: float32 [384, 1472], P(('seq', 'batch')), may hold values from -12 to 12
- inner_weight: float32 [1472, 7168], P(None, ('seq', 'batch')), may hold values from -0.15625 to 0.15625
- inner_first: float32 [1472, 7168], P(None, ('seq', 'batch'))
- inner_second: float32 [1472, 7168], P(None, ('seq', 'batch'))
- inner_average: float32 [1472, 7168], P(None, ('seq', 'batch')), may hold values from -0.15625 to 0.15625
- outer_weight: float32 [3584, 1472], P(('seq', 'batch')), may hold values from -0.09375 to 0.09375
- outer_first: float32 [3584, 1472], P(('seq', 'batch'))
- outer_second: float32 [3584, 1472], P(('seq', 'batch'))
- outer_average: float32 [3584, 1472], P(('seq', 'batch')), may hold values from -0.09375 to 0.09375
- norm_params: float32 [4, 1472], replicated
- norm_first: float32 [4, 1472], replicated
- norm_second: float32 [4, 1472], replicated
- norm_average: float32 [4, 1472], replicated
- bias_table: float32 [6, 32], replicated, may hold values from -4 to 4
- table_first: float32 [6, 32], replicated
- table_second: float32 [6, 32], replicated
- table_average: float32 [6, 32], replicated, may hold values from -4 to 4
Outputs:
- kept_states: bfloat16 [8, 4, 768, 1472], P('batch', 'seq')
- kept_gate: float32 [32, 1024], P('batch', 'seq')
- input_grad: bfloat16 [32, 1024, 1472], P('batch', 'seq')
- attend_updated: float32 [1472, 1152], P(None, ('seq', 'batch'))
- attend_moment: float32 [1472, 1152], P(None, ('seq', 'batch'))
- attend_square: float32 [1472, 1152], P(None, ('seq', 'batch'))
- attend_smooth: float32 [1472, 1152], P(None, ('seq', 'batch'))
- output_updated: float32 [384, 1472], P(('seq', 'batch'))
- output_moment: float32 [384, 1472], P(('seq', 'batch'))
- output_square: float32 [384, 1472], P(('seq', 'batch'))
- output_smooth: float32 [384, 1472], P(('seq', 'batch'))
- inner_updated: float32 [1472, 7168], P(None, ('seq', 'batch'))
- inner_moment: float32 [1472, 7168], P(None, ('seq', 'batch'))
- inner_square: float32 [1472, 7168], P(None, ('seq', 'batch'))
- inner_smooth: float32 [1472, 7168], P(None, ('seq', 'batch'))
- outer_updated: float32 [3584, 1472], P(('seq', 'batch'))
- outer_moment: float32 [3584, 1472], P(('seq', 'batch'))
- outer_square: float32 [3584, 1472], P(('seq', 'batch'))
- outer_smooth: float32 [3584, 1472], P(('seq', 'batch'))
- norm_updated: float32 [4, 1472], replicated
- norm_moment: float32 [4, 1472], replicated
- norm_square: float32 [4, 1472], replicated
- norm_smooth: float32 [4, 1472], replicated
- table_updated: float32 [6, 32], replicated
- table_moment: float32 [6, 32], replicated
- table_square: float32 [6, 32], replicated
- table_smooth: float32 [6, 32], replicated
The draws below stay inside these ranges and needn't reach their ends.
Inputs may be any that keep to these rules, and one draw needn't show every extreme that they name: `keep_mask`: each sequence keeps between 384 and 768 positions, and some sequence keeps exactly 768.
All inputs are finite; a program needn't handle non-finite values.
Results may differ from the reference program's by a relative error of at most 0.015.
Values may be sent and summed in bfloat16 or wider, within the bound.
No kernel may reach another device: no remote copies, remote signals or barrier semaphores. Data moves between devices by JAX's collectives and lax.ppermute only.
A program may use at most 320 MiB of HBM per device.

```python
import math
import jax
import jax.numpy as jnp
from jax import lax

D = 1472
HEADS = 6
HEAD_DIM = 64
FF = 3584
BUCKETS = 32
LEN = 1024
ROWS_DEV = 4
INNER = 384
KEEP_CAP = 768
GROUPS = 8
ROWS = 32
TOKENS = 32768


def moment_pair(key, shape, grad_size):
    first_key, second_key = jax.random.split(key)
    first = jax.random.normal(first_key, shape, jnp.float32) * grad_size / 9.0
    spread = jnp.exp(jax.random.uniform(second_key, shape, jnp.float32, math.log(0.5), math.log(2.0)))
    second = 0.002 * spread * grad_size * grad_size
    return (first, second)


def attend_size():
    return 3.7 * math.sqrt(D * TOKENS / LEN)


def output_size():
    return 0.6 * math.sqrt(TOKENS / LEN)


def inner_size():
    return 0.5 * math.sqrt(D * TOKENS / FF)


def outer_size():
    return 0.5 * math.sqrt(TOKENS)


def table_size():
    return 0.12 * math.sqrt(D * TOKENS)


def norm_size():
    quarter = math.pow(D, -0.25)
    return jnp.array([3.7 * math.sqrt(3 * INNER * TOKENS / (8 * LEN)), 0.45 * math.sqrt(TOKENS), 4.5 * math.sqrt(TOKENS) * quarter, 4.5 * math.sqrt(TOKENS) * quarter], jnp.float32)[:, None]


def norm_rows(key):
    gain_key, vector_key = jax.random.split(key)
    quarter = math.pow(D, -0.25)
    row_scale = jnp.array([1.0, 1.0, quarter], jnp.float32)[:, None]
    gains = (1.0 + jax.random.uniform(gain_key, (3, D), jnp.float32, -0.5, 0.5)) * row_scale
    vector = jax.random.normal(vector_key, (1, D), jnp.float32) * quarter
    return jnp.concatenate([gains, vector], axis=0)


def draw_keep_mask(key, part):
    count_key, full_key, order_key = jax.random.split(jax.random.fold_in(key, 40), 3)
    counts = jax.random.randint(count_key, (ROWS,), KEEP_CAP // 2, KEEP_CAP + 1)
    full_row = jax.random.randint(full_key, (), 0, ROWS)
    counts = jnp.where(jnp.arange(ROWS) == full_row, KEEP_CAP, counts)
    orders = jax.vmap(lambda row_key: jax.random.permutation(row_key, LEN))(jax.random.split(order_key, ROWS))
    ranks = jnp.argsort(orders, axis=1, stable=True)
    return (ranks < counts[:, None]).astype(jnp.int32)


def draw_attend_first(key, part):
    return moment_pair(jax.random.fold_in(key, 1), (D, 3 * INNER), attend_size())[0]


def draw_attend_second(key, part):
    return moment_pair(jax.random.fold_in(key, 1), (D, 3 * INNER), attend_size())[1]


def draw_output_first(key, part):
    return moment_pair(jax.random.fold_in(key, 2), (INNER, D), output_size())[0]


def draw_output_second(key, part):
    return moment_pair(jax.random.fold_in(key, 2), (INNER, D), output_size())[1]


def draw_inner_first(key, part):
    return moment_pair(jax.random.fold_in(key, 3), (D, 2 * FF), inner_size())[0]


def draw_inner_second(key, part):
    return moment_pair(jax.random.fold_in(key, 3), (D, 2 * FF), inner_size())[1]


def draw_outer_first(key, part):
    return moment_pair(jax.random.fold_in(key, 4), (FF, D), outer_size())[0]


def draw_outer_second(key, part):
    return moment_pair(jax.random.fold_in(key, 4), (FF, D), outer_size())[1]


def draw_norm_first(key, part):
    return moment_pair(jax.random.fold_in(key, 5), (4, D), norm_size())[0]


def draw_norm_second(key, part):
    return moment_pair(jax.random.fold_in(key, 5), (4, D), norm_size())[1]


def draw_table_first(key, part):
    return moment_pair(jax.random.fold_in(key, 6), (HEADS, BUCKETS), table_size())[0]


def draw_table_second(key, part):
    return moment_pair(jax.random.fold_in(key, 6), (HEADS, BUCKETS), table_size())[1]


def draw_norm_params(key, part):
    return norm_rows(jax.random.fold_in(key, 7))


def draw_norm_average(key, part):
    return norm_rows(jax.random.fold_in(key, 8))


def block_levels(key, shape, shards, smallest, largest):
    level = 1.0
    for position, shards_of in shards:
        draws = jax.random.uniform(jax.random.fold_in(jax.random.fold_in(key, 6), position), (shards_of,), jnp.float32, smallest / len(shards), largest / len(shards))
        level = level * jnp.repeat(jnp.exp(draws), shape[position] // shards_of).reshape((-1,) + (1,) * (len(shape) - 1 - position))
    return level


def bell_draw(key, dims, width, reach, pieces=(), held_as=jnp.bfloat16):
    drawn = width * jax.random.normal(key, dims, jnp.float32)
    if pieces:
        drawn = drawn * block_levels(key, dims, pieces, -0.22, 0.18)
    return jnp.clip(drawn, -reach, reach).astype(held_as)


def setup_inputs(seed: int = 0) -> dict:
    key_list = jax.random.split(jax.random.key(seed), 30)
    hidden = bell_draw(key_list[0], (ROWS, LEN, D), 1.0, 6.0, ((0, 8), (1, 4)))
    keep_mask = draw_keep_mask(jax.random.fold_in(key_list[29], 71), 0)
    states_cotangent = bell_draw(key_list[2], (GROUPS, ROWS_DEV, KEEP_CAP, D), 1.0, 6.0, ((0, 8), (1, 4)))
    gate_cotangent = bell_draw(key_list[3], (ROWS, LEN), 1.0, 6.0, ((0, 8), (1, 4)), jnp.float32)
    step_count = jax.random.randint(key_list[4], (1,), 2, 21).astype(jnp.int32)
    attend_weight = bell_draw(key_list[5], (D, 3 * INNER), (8 * D) ** -0.5, 0.0546875, ((1, 32),), jnp.float32)
    attend_first = draw_attend_first(jax.random.fold_in(key_list[29], 71), 0)
    attend_second = draw_attend_second(jax.random.fold_in(key_list[29], 71), 0)
    attend_average = bell_draw(key_list[8], (D, 3 * INNER), (8 * D) ** -0.5, 0.0546875, ((1, 32),), jnp.float32)
    output_weight = bell_draw(key_list[9], (INNER, D), 2.0, 12.0, ((0, 32),), jnp.float32)
    output_first = draw_output_first(jax.random.fold_in(key_list[29], 71), 0)
    output_second = draw_output_second(jax.random.fold_in(key_list[29], 71), 0)
    output_average = bell_draw(key_list[12], (INNER, D), 2.0, 12.0, ((0, 32),), jnp.float32)
    inner_weight = bell_draw(key_list[13], (D, 2 * FF), D ** -0.5, 0.15625, ((1, 32),), jnp.float32)
    inner_first = draw_inner_first(jax.random.fold_in(key_list[29], 71), 0)
    inner_second = draw_inner_second(jax.random.fold_in(key_list[29], 71), 0)
    inner_average = bell_draw(key_list[16], (D, 2 * FF), D ** -0.5, 0.15625, ((1, 32),), jnp.float32)
    outer_weight = bell_draw(key_list[17], (FF, D), FF ** -0.5, 0.09375, ((0, 32),), jnp.float32)
    outer_first = draw_outer_first(jax.random.fold_in(key_list[29], 71), 0)
    outer_second = draw_outer_second(jax.random.fold_in(key_list[29], 71), 0)
    outer_average = bell_draw(key_list[20], (FF, D), FF ** -0.5, 0.09375, ((0, 32),), jnp.float32)
    norm_params = draw_norm_params(jax.random.fold_in(key_list[29], 71), 0)
    norm_first = draw_norm_first(jax.random.fold_in(key_list[29], 71), 0)
    norm_second = draw_norm_second(jax.random.fold_in(key_list[29], 71), 0)
    norm_average = draw_norm_average(jax.random.fold_in(key_list[29], 71), 0)
    bias_table = bell_draw(key_list[25], (HEADS, BUCKETS), 0.7, 4.0, (), jnp.float32)
    table_first = draw_table_first(jax.random.fold_in(key_list[29], 71), 0)
    table_second = draw_table_second(jax.random.fold_in(key_list[29], 71), 0)
    table_average = bell_draw(key_list[28], (HEADS, BUCKETS), 0.7, 4.0, (), jnp.float32)
    return dict(hidden=hidden, keep_mask=keep_mask, states_cotangent=states_cotangent, gate_cotangent=gate_cotangent, step_count=step_count, attend_weight=attend_weight, attend_first=attend_first, attend_second=attend_second, attend_average=attend_average, output_weight=output_weight, output_first=output_first, output_second=output_second, output_average=output_average, inner_weight=inner_weight, inner_first=inner_first, inner_second=inner_second, inner_average=inner_average, outer_weight=outer_weight, outer_first=outer_first, outer_second=outer_second, outer_average=outer_average, norm_params=norm_params, norm_first=norm_first, norm_second=norm_second, norm_average=norm_average, bias_table=bias_table, table_first=table_first, table_second=table_second, table_average=table_average)


@jax.custom_vjp
def low(v):
    return lax.optimization_barrier(v.astype(jnp.bfloat16)).astype(jnp.float32)

@jax.custom_vjp
def low_back(v):
    return v

def low_keep(v):
    return (low(v), None)

def low_pass(kept, grad):
    return (grad,)

def back_keep(v):
    return (v, None)

def back_low(kept, grad):
    return (low(grad),)
low.defvjp(low_keep, low_pass)
low_back.defvjp(back_keep, back_low)
EPSILON = 1e-06
GATE_RANGE = -30.0
MOMENT_DECAY = 0.9
SQUARE_DECAY = 0.999
ADAM_FLOOR = 1e-08
WEIGHT_DECAY = 0.01
RATE_ATTEND = 0.02
RATE_OUTPUT = 4.0
RATE_INNER = 0.06
RATE_OUTER = 0.04
RATE_NORM = 0.5
RATE_TABLE = 1.0
far_edges = (12, 16, 23, 32, 46, 64, 91)
PRECISE = lax.Precision.HIGHEST

def rms_scale(values):
    return lax.rsqrt(lax.optimization_barrier(jnp.mean(values * values, axis=-1, keepdims=True)) + EPSILON)

def bucket_of(query_pos, key_pos):
    offset = key_pos[None, :] - query_pos[:, None]
    distance = jnp.abs(offset)
    far_bucket = jnp.full(distance.shape, 8, jnp.int32)
    for edge_value in far_edges:
        far_bucket = far_bucket + (distance >= edge_value).astype(jnp.int32)
    near_bucket = jnp.where(distance < 8, distance, far_bucket)
    return (near_bucket + jnp.where(offset > 0, 16, 0)).astype(jnp.int32)

def row_take(values, index):
    return jnp.take(values, index, axis=0)

def plain_dot(left, right):
    return jnp.dot(left, right, precision=PRECISE, preferred_element_type=jnp.float32)

def adam_step(weight, first, second, grad, rate, bias_one, bias_two, average, smooth_decay):
    first_new = MOMENT_DECAY * first + (1.0 - MOMENT_DECAY) * grad
    second_new = SQUARE_DECAY * second + (1.0 - SQUARE_DECAY) * grad * grad
    direction = first_new / bias_one / (jnp.sqrt(second_new / bias_two) + ADAM_FLOOR)
    weight_new = weight - rate * (direction + WEIGHT_DECAY * weight)
    average_new = smooth_decay * average + (1.0 - smooth_decay) * weight_new
    return (weight_new, first_new, second_new, average_new)

def reference(hidden, keep_mask, states_cotangent, gate_cotangent, step_count, attend_weight, attend_first, attend_second, attend_average, output_weight, output_first, output_second, output_average, inner_weight, inner_first, inner_second, inner_average, outer_weight, outer_first, outer_second, outer_average, norm_params, norm_first, norm_second, norm_average, bias_table, table_first, table_second, table_average):
    keep_float = keep_mask.astype(jnp.float32)
    positions = jnp.arange(LEN, dtype=jnp.int32)
    row_index = jnp.arange(ROWS, dtype=jnp.int32)[:, None]
    kept_rank = (jnp.cumsum(keep_mask, axis=1) - 1).astype(jnp.int32)
    slot_target = jnp.where(keep_mask > 0, kept_rank, KEEP_CAP).astype(jnp.int32)
    slot_source = jnp.zeros((ROWS, KEEP_CAP), jnp.int32).at[row_index, slot_target].set(jnp.broadcast_to(positions, (ROWS, LEN)), mode='drop')
    slot_valid = (jnp.arange(KEEP_CAP, dtype=jnp.int32)[None, :] < lax.optimization_barrier(jnp.sum(keep_mask, axis=1)).astype(jnp.int32)[:, None]).astype(jnp.float32)
    bucket_grid = bucket_of(positions, positions)

    def forward(hidden_full, attend_master, output_master, inner_master, outer_master, norm_values, table_values):
        attend_low = low(attend_master)
        output_low = low(output_master)
        inner_low = low(inner_master)
        outer_low = low(outer_master)
        bias_full = table_values[:, bucket_grid]

        def one_row(row_in):
            normed = low(row_in * rms_scale(row_in) * norm_values[0])
            projected = low(low_back(plain_dot(normed, attend_low)))
            queries = projected[:, :INNER].reshape(LEN, HEADS, HEAD_DIM)
            keys_row = projected[:, INNER:2 * INNER].reshape(LEN, HEADS, HEAD_DIM)
            values_row = projected[:, 2 * INNER:].reshape(LEN, HEADS, HEAD_DIM)
            scores = jnp.einsum('qhd,khd->hqk', queries, keys_row, precision=PRECISE) + bias_full
            scores = low_back(scores)
            probs = jax.nn.softmax(scores, axis=-1)
            mixed = jnp.einsum('hqk,khd->qhd', low(probs), values_row, precision=PRECISE).reshape(LEN, INNER)
            mixed = low(low_back(mixed))
            middle = row_in + low_back(plain_dot(mixed, output_low))
            normed_two = low(middle * rms_scale(middle) * norm_values[1])
            lifted = low_back(plain_dot(normed_two, inner_low))
            units = low(jax.nn.gelu(lifted[:, :FF], approximate=True) * lifted[:, FF:])
            result = middle + low_back(plain_dot(units, outer_low))
            gate_in = result * rms_scale(result) * norm_values[2]
            logits = jnp.dot(gate_in, norm_values[3], precision=PRECISE)
            return (low(result), GATE_RANGE * jax.nn.sigmoid(logits))
        lowered, gates = lax.map(jax.checkpoint(one_row), hidden_full)
        kept = jax.vmap(row_take)(lowered, slot_source) * slot_valid[:, :, None]
        return (kept, gates * keep_float)
    (kept, gated), pull_back = jax.vjp(forward, hidden.astype(jnp.float32), attend_weight, output_weight, inner_weight, outer_weight, norm_params, bias_table)
    grads = pull_back((states_cotangent.astype(jnp.float32).reshape(ROWS, KEEP_CAP, D), gate_cotangent))
    steps_done = step_count[0].astype(jnp.float32)
    bias_one = 1.0 - MOMENT_DECAY ** steps_done
    bias_two = 1.0 - SQUARE_DECAY ** steps_done
    smooth_decay = (1.0 + steps_done) / (10.0 + steps_done)
    attend_new = adam_step(attend_weight, attend_first, attend_second, grads[1], RATE_ATTEND, bias_one, bias_two, attend_average, smooth_decay)
    output_new = adam_step(output_weight, output_first, output_second, grads[2], RATE_OUTPUT, bias_one, bias_two, output_average, smooth_decay)
    inner_new = adam_step(inner_weight, inner_first, inner_second, grads[3], RATE_INNER, bias_one, bias_two, inner_average, smooth_decay)
    outer_new = adam_step(outer_weight, outer_first, outer_second, grads[4], RATE_OUTER, bias_one, bias_two, outer_average, smooth_decay)
    norm_new = adam_step(norm_params, norm_first, norm_second, grads[5], RATE_NORM, bias_one, bias_two, norm_average, smooth_decay)
    table_new = adam_step(bias_table, table_first, table_second, grads[6], RATE_TABLE, bias_one, bias_two, table_average, smooth_decay)
    kept_states = kept.astype(jnp.bfloat16).reshape(GROUPS, ROWS_DEV, KEEP_CAP, D)
    input_grad = grads[0].astype(jnp.bfloat16)
    return (kept_states, gated, input_grad, attend_new[0], attend_new[1], attend_new[2], attend_new[3], output_new[0], output_new[1], output_new[2], output_new[3], inner_new[0], inner_new[1], inner_new[2], inner_new[3], outer_new[0], outer_new[1], outer_new[2], outer_new[3], norm_new[0], norm_new[1], norm_new[2], norm_new[3], table_new[0], table_new[1], table_new[2], table_new[3])
```

```python
import functools

import jax
import jax.numpy as jnp
from jax import lax
from jax.experimental import pallas as pl
from jax.experimental.pallas import tpu as pltpu
from jax.sharding import PartitionSpec as P

D = 1472
HEADS = 6
HEAD_DIM = 64
FF = 3584
BUCKETS = 32
LEN = 1024
INNER = 384
KEEP_CAP = 768


EPSILON = 1e-06
GATE_RANGE = -30.0
MOMENT_DECAY = 0.9
SQUARE_DECAY = 0.999
ADAM_FLOOR = 1e-08
WEIGHT_DECAY = 0.01
RATE_ATTEND = 0.02
RATE_OUTPUT = 4.0
RATE_INNER = 0.06
RATE_OUTER = 0.04
RATE_NORM = 0.5
RATE_TABLE = 1.0
far_edges = (12, 16, 23, 32, 46, 64, 91)
AXES = ("y", "core", "batch")
FREE = pl.CostEstimate(flops=0, bytes_accessed=0, transcendentals=0)
QB = 256
WB = 2048
MIB = 2**20
NT = (((1,), (1,)), ((), ()))
TN = (((0,), (0,)), ((), ()))


def cost(micros):
    return pl.CostEstimate(flops=micros * 10**9, bytes_accessed=0, transcendentals=0)


def mm(a,b,dims=(((1,),(0,)),((),()))):
    return lax.dot_general(a,b,dims,preferred_element_type=jnp.float32)
def head_mask(shape,h):
    lane=lax.broadcasted_iota(jnp.int32,shape,1)
    return (lane<64) if h==0 else (lane>=64)
def fill_bias(t_ref,b_ref):
    for h in range(2):
        row=jnp.broadcast_to(t_ref[0,h:h+1,:],(QB,WB))
        b_ref[h]=pltpu.roll(row,0,1,stride=1,stride_axis=0)
def fwd_kernel(q_ref,k_ref,v_ref,t_ref,o_ref,l_ref,b_ref):
    fill_bias(t_ref,b_ref)
    k=k_ref[...]; v=v_ref[...]
    nq=LEN//QB
    def body(i,_):
        rows=pl.ds(pl.multiple_of(i*QB,QB),QB)
        qb=q_ref[rows,:]
        cols=pl.ds(pl.multiple_of((nq-1-i)*QB,QB),LEN)
        outs=[];ls=[]
        for h in range(2):
            qm=jnp.where(head_mask(qb.shape,h),qb,jnp.zeros_like(qb))
            s=mm(qm,k,NT)+b_ref[h,:,cols]
            m=jnp.max(s,-1,keepdims=True)
            e=jnp.exp(s-m)
            l=jnp.sum(e,-1,keepdims=True)
            o=mm((e*(1.0/l)).astype(jnp.bfloat16),v)
            outs.append(o); ls.append(m+jnp.log(l))
        msk=head_mask(outs[0].shape,0)
        o_ref[rows,:]=jnp.where(msk,outs[0],outs[1]).astype(o_ref.dtype)
        l_ref[rows,:]=jnp.where(msk,jnp.broadcast_to(ls[0],outs[0].shape),jnp.broadcast_to(ls[1],outs[0].shape))
        return 0
    lax.fori_loop(0,nq,body,0)
def attn_fwd(qkv,tvec):
    n=INNER//128
    return pl.pallas_call(fwd_kernel,grid=(n,),
        in_specs=[pl.BlockSpec((LEN,128),lambda h:(0,h)),pl.BlockSpec((LEN,128),lambda h:(0,n+h)),pl.BlockSpec((LEN,128),lambda h:(0,2*n+h)),
                  pl.BlockSpec((1,2,WB),lambda h:(h,0,0))],
        out_specs=[pl.BlockSpec((LEN,128),lambda h:(0,h)),pl.BlockSpec((LEN,128),lambda h:(0,h))],
        out_shape=[jax.ShapeDtypeStruct((LEN,INNER),jnp.bfloat16),jax.ShapeDtypeStruct((LEN,INNER),jnp.float32)],
        scratch_shapes=[pltpu.VMEM((2,QB,WB),jnp.float32)],
        compiler_params=pltpu.CompilerParams(vmem_limit_bytes=48*2**20),
        cost_estimate=cost(20),
        name="attn_fwd")(qkv,qkv,qkv,tvec)
def bwd_kernel(q_ref,k_ref,v_ref,g_ref,l_ref,t_ref,o_ref,dt_ref,b_ref,db_ref,dk_ref,dv_ref):
    fill_bias(t_ref,b_ref)
    db_ref[...]=jnp.zeros_like(db_ref)
    dk_ref[...]=jnp.zeros_like(dk_ref)
    dv_ref[...]=jnp.zeros_like(dv_ref)
    k=k_ref[...]; v=v_ref[...]
    nq=LEN//QB
    hp=pl.program_id(0)
    def body(i,_):
        rows=pl.ds(pl.multiple_of(i*QB,QB),QB)
        qb=q_ref[rows,:]; gb=g_ref[rows,:]; lb=l_ref[rows,:]
        cols=pl.ds(pl.multiple_of((nq-1-i)*QB,QB),LEN)
        dqs=[]
        for h in range(2):
            hm=head_mask(qb.shape,h)
            qm=jnp.where(hm,qb,jnp.zeros_like(qb)); gm=jnp.where(hm,gb,jnp.zeros_like(gb))
            s=mm(qm,k,NT)+b_ref[h,:,cols]
            p=jnp.exp(s-lb[:,64*h:64*h+1])
            dp=mm(gm,v,NT)
            t=p*dp
            d=jnp.sum(t,-1,keepdims=True)
            ds=(t-p*d)
            db_ref[h,:,cols]+=ds
            ds=ds.astype(jnp.bfloat16)
            dv_ref[...]+=mm(p.astype(jnp.bfloat16),gm,TN)
            dk_ref[...]+=mm(ds,qm,TN)
            dqs.append(mm(ds,k))
        o_ref[rows,pl.ds(pl.multiple_of(hp*128,128),128)]=jnp.where(head_mask(dqs[0].shape,0),dqs[0],dqs[1]).astype(o_ref.dtype)
        return 0
    lax.fori_loop(0,nq,body,0)
    o_ref[:,pl.ds(pl.multiple_of(INNER+hp*128,128),128)]=dk_ref[...].astype(o_ref.dtype)
    o_ref[:,pl.ds(pl.multiple_of(2*INNER+hp*128,128),128)]=dv_ref[...].astype(o_ref.dtype)
    for h in range(2):
        rows=QB//2
        while rows>=8:
            db_ref[h,:rows,:]=db_ref[h,:rows,:]+pltpu.roll(db_ref[h,rows:2*rows,:],WB-rows,1)
            rows//=2
        dt_ref[0,h]=db_ref[h,:8,:]
def attn_bwd(qkv,grad,lse,tvec):
    n=INNER//128
    return pl.pallas_call(bwd_kernel,grid=(n,),
        in_specs=[pl.BlockSpec((LEN,128),lambda h:(0,h)),pl.BlockSpec((LEN,128),lambda h:(0,n+h)),pl.BlockSpec((LEN,128),lambda h:(0,2*n+h)),
                  pl.BlockSpec((LEN,128),lambda h:(0,h)),pl.BlockSpec((LEN,128),lambda h:(0,h)),
                  pl.BlockSpec((1,2,WB),lambda h:(h,0,0))],
        out_specs=[pl.BlockSpec((LEN,3*INNER),lambda h:(0,0)),pl.BlockSpec((1,2,8,WB),lambda h:(h,0,0,0))],
        out_shape=[jax.ShapeDtypeStruct((LEN,3*INNER),jnp.bfloat16),jax.ShapeDtypeStruct((n,2,8,WB),jnp.float32)],
        scratch_shapes=[pltpu.VMEM((2,QB,WB),jnp.float32),pltpu.VMEM((2,QB,WB),jnp.float32),pltpu.VMEM((LEN,128),jnp.float32),pltpu.VMEM((LEN,128),jnp.float32)],
        compiler_params=pltpu.CompilerParams(vmem_limit_bytes=48*2**20),
        cost_estimate=cost(34),
        name="attn_bwd")(qkv,qkv,qkv,grad,lse,tvec)


def bucket_of_offset(offset):
    distance = jnp.abs(offset)
    far_bucket = jnp.full(distance.shape, 8, jnp.int32)
    for edge_value in far_edges:
        far_bucket = far_bucket + (distance >= edge_value).astype(jnp.int32)
    near_bucket = jnp.where(distance < 8, distance, far_bucket)
    return near_bucket + jnp.where(offset > 0, 16, 0)


def adam_step(weight, first, second, grad, rate, bias_one, bias_two, average, smooth_decay):
    first_new = MOMENT_DECAY * first + (1.0 - MOMENT_DECAY) * grad
    second_new = SQUARE_DECAY * second + (1.0 - SQUARE_DECAY) * grad * grad
    direction = first_new / bias_one / (jnp.sqrt(second_new / bias_two) + ADAM_FLOOR)
    weight_new = weight - rate * (direction + WEIGHT_DECAY * weight)
    average_new = smooth_decay * average + (1.0 - smooth_decay) * weight_new
    return (weight_new, first_new, second_new, average_new)


def low(values):
    return values.astype(jnp.bfloat16)


def wide(values):
    return values.astype(jnp.float32)


def tie(*values):
    return lax.optimization_barrier(values)


class Grid:
    def __init__(self, seq_count, batch_count):
        if batch_count == 8:
            digits = [4, 2]
        else:
            digits, rest = [], batch_count
            while rest % 4 == 0:
                digits, rest = [4] + digits, rest // 4
            if rest > 1:
                digits = [rest] + digits
        self.sizes = [seq_count // 2, 2] + digits
        self.total = seq_count * batch_count
        self.batch_dims = list(range(2, len(self.sizes)))
        self.swaps = self.sizes[-1] == self.sizes[0]

    def split(self, index):
        out = []
        for size in reversed(self.sizes):
            out.append(index % size)
            index = index // size
        return out[::-1]

    def join(self, coords):
        index = 0
        for size, coord in zip(self.sizes, coords):
            index = index * size + coord
        return index

    def shift(self, values, dim, step, odd_dim=None):
        pairs = []
        for index in range(self.total):
            coords = self.split(index)
            along = dim if odd_dim is None or coords[1] == 0 else odd_dim
            coords[along] = (coords[along] + step) % self.sizes[along]
            pairs.append((index, self.join(coords)))
        return lax.ppermute(values, AXES, pairs)

    def mine(self):
        return self.split(lax.axis_index(AXES))

    def small_stages(self):
        first = [(dim, dim) for dim in self.batch_dims[:-1]]
        x, y = self.batch_dims[-1], 0
        if self.swaps:
            return first + [(x, y), (y, x), (1, 1)]
        return first + [(x, x), (y, y), (1, 1)]

    def small_owner(self):
        stages = self.small_stages()
        rest = jnp.arange(self.total, dtype=jnp.int32)
        steps = []
        for dim, _ in stages:
            steps.append(rest % self.sizes[dim])
            rest = rest // self.sizes[dim]
        mine = self.mine()
        core = (mine[1] + steps[-1]) % 2
        coords = list(mine)
        coords[1] = core
        for (dim, odd_dim), step in zip(stages[:-1], steps[:-1]):
            if dim == odd_dim:
                coords[dim] = (coords[dim] - step) % self.sizes[dim]
            else:
                for this, other in ((dim, 0), (odd_dim, 1)):
                    coords[this] = jnp.where(
                        core == other, (coords[this] - step) % self.sizes[this], coords[this]
                    )
        return self.join(coords)


def absolute(parts, place):
    count = len(parts)
    if count == 2:
        first = place == 0
        return [jnp.where(first, parts[0], parts[1]), jnp.where(first, parts[1], parts[0])]
    return [
        lax.select_n(lax.rem(place - j + count, count), *parts) for j in range(count)
    ]


class Scatter:
    def __init__(self, grid, pieces, order):
        self.grid = grid
        self.plan = list(order)
        self.sent = False
        self.start(pieces)

    def start(self, pieces):
        dim = self.plan[0]
        count = self.grid.sizes[dim]
        axis = max(dim - 1, 0)
        place = self.grid.mine()[dim]
        if count == 2:
            parts = [lax.slice_in_dim(pieces, j, j + 1, axis=axis) for j in range(count)]
            self.parts = absolute(parts, place)
        else:
            self.parts = [
                lax.dynamic_slice_in_dim(pieces, lax.rem(place - j + count, count), 1, axis)
                for j in range(count)
            ]

    def settle(self):
        self.plan.pop(0)
        total = wide(self.parts[0])
        for part in self.parts[1:]:
            total = total + wide(part)
        self.total = low(total) if self.plan else total
        self.sent = False
        if self.plan:
            self.start(self.total)

    def send(self):
        dim = self.plan[0]
        for step in range(1, len(self.parts)):
            self.parts[step] = self.grid.shift(self.parts[step], dim, -step)
        self.sent = True

    def advance(self, *values):
        if self.sent:
            _, *self.parts = tie(values[0], *self.parts)
            self.settle()
        if self.plan:
            count = len(self.parts) - 1
            tied = tie(*values, *self.parts[1:])
            self.parts[1:] = tied[-count:]
            values = tied[:-count]
            self.send()
        return values[0] if len(values) == 1 else values

    def result(self, value):
        if self.sent:
            _, *self.parts = tie(value, *self.parts)
        while self.plan:
            if self.sent:
                self.settle()
            if self.plan:
                self.send()
        return self.total


def exchange(values):
    return lax.all_to_all(values, ("y", "core"), split_axis=0, concat_axis=0, tiled=True)


def pick(near_ref, far_ref):
    step = pl.program_id(0)
    return jnp.where(step < pl.num_programs(0) // 2, near_ref[...], far_ref[...])


def pair_specs(rows, blocks):
    return [
        pl.BlockSpec((rows, QB), lambda t, core: (0, jnp.minimum(t, blocks - 1))),
        pl.BlockSpec((rows, QB), lambda t, core: (0, jnp.maximum(t - blocks, 0))),
    ]


def by_core(kernel, grid, in_specs, out_specs, out_shape, name, micros):
    return pl.pallas_call(
        lambda core_ref, *refs: kernel(*refs),
        grid_spec=pltpu.PrefetchScalarGridSpec(
            num_scalar_prefetch=1, grid=grid, in_specs=in_specs, out_specs=out_specs
        ),
        out_shape=out_shape,
        compiler_params=pltpu.CompilerParams(vmem_limit_bytes=56 * MIB),
        cost_estimate=cost(micros),
        name=name,
    )


def weight_spec(first):
    return pl.BlockSpec((1, FF // 2, D), lambda t, core: (first + core[0], 0, 0))


def token_spec(rows, first=0):
    return pl.BlockSpec((rows, QB), lambda t, core: (0, first + t))


def lift_kernel(near_ref, far_ref, g_ref, u_ref, units_ref, da_ref, db_ref):
    block = pick(near_ref, far_ref)
    rows = units_ref.shape[0] // 2
    for part in range(2):
        here = slice(part * rows, (part + 1) * rows)
        gate = mm(g_ref[0, here, :], block)
        up = mm(u_ref[0, here, :], block)
        root = 0.7978845608028654
        square = gate * gate
        inside = jnp.tanh(root * gate * (1.0 + 0.044715 * square))
        half = 0.5 * (1.0 + inside)
        active = gate * half
        slope = half + 0.5 * gate * (1.0 - inside * inside) * (
            root * (1.0 + 3.0 * 0.044715 * square)
        )
        units_ref[here, :] = low(active * up)
        da_ref[here, :] = low(up * slope)
        db_ref[here, :] = low(active)


def lift(core, near, far, inner_full):
    tokens = 2 * near.shape[1]
    blocks = near.shape[1] // QB
    out = jax.ShapeDtypeStruct((FF // 2, tokens), jnp.bfloat16)
    return by_core(
        lift_kernel,
        (2 * blocks,),
        pair_specs(D, blocks) + [weight_spec(0), weight_spec(2)],
        [token_spec(FF // 2)] * 3,
        [out] * 3,
        "lift",
        40,
    )(core, near, far, inner_full, inner_full)


def unlift_kernel(near_ref, far_ref, w_ref, da_ref, db_ref, out_ref):
    half = w_ref.shape[1]
    units_grad = mm(w_ref[0], pick(near_ref, far_ref))
    out_ref[:half, :] = low(units_grad * wide(da_ref[...]))
    out_ref[half:, :] = low(units_grad * wide(db_ref[...]))


def unlift(core, near, far, outer_full, slope_gate, slope_up):
    tokens = 2 * near.shape[1]
    blocks = near.shape[1] // QB
    return by_core(
        unlift_kernel,
        (2 * blocks,),
        pair_specs(D, blocks) + [weight_spec(0)] + [token_spec(FF // 2)] * 2,
        token_spec(FF),
        jax.ShapeDtypeStruct((FF, tokens), jnp.bfloat16),
        "unlift",
        20,
    )(core, near, far, outer_full, slope_gate, slope_up)


def lower_kernel(w_ref, units_ref, out_ref):
    out_ref[...] = mm(w_ref[0], units_ref[...], TN).astype(out_ref.dtype)


def lower(core, outer_full, units, first, dtype):
    tokens = units.shape[1] // 2
    return by_core(
        lower_kernel,
        (tokens // QB,),
        [weight_spec(0), token_spec(FF // 2, first * (tokens // QB))],
        token_spec(D),
        jax.ShapeDtypeStruct((D, tokens), dtype),
        "lower",
        11,
    )(core, outer_full, units)


def states_grad_kernel(g_ref, u_ref, grad_ref, out_ref):
    half = g_ref.shape[1]
    total = mm(g_ref[0], grad_ref[:half, :], TN)
    out_ref[...] = (total + mm(u_ref[0], grad_ref[half:, :], TN)).astype(out_ref.dtype)


def states_grad(core, inner_full, lifted_grad, first, dtype):
    tokens = lifted_grad.shape[1] // 2
    return by_core(
        states_grad_kernel,
        (tokens // QB,),
        [weight_spec(0), weight_spec(2), token_spec(FF, first * (tokens // QB))],
        token_spec(D),
        jax.ShapeDtypeStruct((D, tokens), dtype),
        "states_grad",
        19,
    )(core, inner_full, inner_full, lifted_grad)


def whole(shape):
    return pl.BlockSpec(shape, lambda *_: (0,) * len(shape))


def weight_grad_kernel(block, half, left_ref, near_ref, far_ref, out_ref):
    tokens = near_ref.shape[1]
    left = left_ref[...]
    if half is not None:
        starts = range(half * (block // 2), left.shape[0], block)
        left = jnp.concatenate([left[start : start + block // 2] for start in starts], axis=0)
    total = mm(left[:, :tokens], near_ref[...], NT)
    out_ref[...] = low(total + mm(left[:, tokens:], far_ref[...], NT))


def weight_grad(left, near, far, count, block=None, half=None):
    tokens = near.shape[1]
    tile = left.shape[0] // count
    rows = tile if half is None else tile // 2
    return pl.pallas_call(
        functools.partial(weight_grad_kernel, block, half),
        grid=(count,),
        in_specs=[
            pl.BlockSpec((tile, 2 * tokens), lambda f: (f, 0)),
            whole((D, tokens)),
            whole((D, tokens)),
        ],
        out_specs=pl.BlockSpec((rows, D), lambda f: (f, 0)),
        out_shape=jax.ShapeDtypeStruct((count * rows, D), jnp.bfloat16),
        compiler_params=pltpu.CompilerParams(vmem_limit_bytes=56 * MIB),
        cost_estimate=cost(4 * count),
        name="weight_grad",
    )(left, near, far)


def spread_kernel(rank_ref, cot_ref, out_ref):
    slot = lax.broadcasted_iota(jnp.int32, (KEEP_CAP, QB), 0)
    chosen = low(jnp.where(slot == rank_ref[0], 1.0, 0.0))
    out_ref[0] = low(mm(cot_ref[...], chosen))


def spread(rank, cotangent):
    blocks = rank.shape[0]
    return pl.pallas_call(
        spread_kernel,
        grid=(blocks,),
        in_specs=[
            pl.BlockSpec((1, 1, QB), lambda i: (i, 0, 0)),
            pl.BlockSpec((D, KEEP_CAP), lambda i: (0, 0)),
        ],
        out_specs=pl.BlockSpec((1, D, QB), lambda i: (i, 0, 0)),
        out_shape=jax.ShapeDtypeStruct((blocks, D, QB), jnp.bfloat16),
        compiler_params=pltpu.CompilerParams(vmem_limit_bytes=40 * MIB),
        cost_estimate=cost(4),
        name="spread",
    )(rank, cotangent)


def compact_kernel(rank_ref, rows_ref, out_ref, sum_ref):
    slot = lax.broadcasted_iota(jnp.int32, (QB, KEEP_CAP), 1)
    chosen = low(jnp.where(slot == rank_ref[0], 1.0, 0.0))
    part = mm(rows_ref[0], chosen)

    @pl.when(pl.program_id(0) == 0)
    def _():
        sum_ref[...] = part

    @pl.when(pl.program_id(0) > 0)
    def _():
        sum_ref[...] += part

    @pl.when(pl.program_id(0) == pl.num_programs(0) - 1)
    def _():
        out_ref[...] = low(sum_ref[...])


def compact(rank, rows):
    blocks = rank.shape[0]
    return pl.pallas_call(
        compact_kernel,
        grid=(blocks,),
        in_specs=[
            pl.BlockSpec((1, QB, 1), lambda i: (i, 0, 0)),
            pl.BlockSpec((1, D, QB), lambda i: (i, 0, 0)),
        ],
        out_specs=pl.BlockSpec((D, KEEP_CAP), lambda i: (0, 0)),
        out_shape=jax.ShapeDtypeStruct((D, KEEP_CAP), jnp.bfloat16),
        scratch_shapes=[pltpu.VMEM((D, KEEP_CAP), jnp.float32)],
        compiler_params=pltpu.CompilerParams(vmem_limit_bytes=40 * MIB),
        cost_estimate=cost(6),
        name="compact",
    )(rank, rows)


def per_device(
    seq_count,
    batch_count,
    hidden,
    keep_mask,
    states_cotangent,
    gate_cotangent,
    step_count,
    attend_weight,
    attend_first,
    attend_second,
    attend_average,
    output_weight,
    output_first,
    output_second,
    output_average,
    inner_weight,
    inner_first,
    inner_second,
    inner_average,
    outer_weight,
    outer_first,
    outer_second,
    outer_average,
    norm_params,
    norm_first,
    norm_second,
    norm_average,
    bias_table,
    table_first,
    table_second,
    table_average,
):
    grid = Grid(seq_count, batch_count)
    batch_dims = grid.batch_dims
    batch_sizes = [grid.sizes[dim] for dim in batch_dims]
    ones = (1,) * len(batch_dims)
    seq_place = lax.axis_index(("y", "core"))
    row_count, shard_len = hidden.shape[0], hidden.shape[1]
    tokens = row_count * shard_len
    attend_rows, output_rows = attend_weight.shape[1], output_weight.shape[0]
    inner_rows, outer_rows = inner_weight.shape[1], outer_weight.shape[0]
    half_ff = FF // 2

    core = lax.axis_index("core").reshape(1).astype(jnp.int32)
    small_rows = attend_rows + output_rows
    small = jnp.concatenate([low(attend_weight).T, low(output_weight)], axis=0)
    small = lax.all_gather(small, AXES, axis=0)
    attend_full = small[:, :attend_rows].reshape(3 * INNER, D)
    output_full = small[:, attend_rows:].reshape(INNER, D)
    inner_full = lax.all_gather(low(inner_weight).T, AXES, axis=0, tiled=True)
    inner_full = inner_full.reshape(4, FF // 2, D)
    swapped = []
    for index in range(grid.total):
        y, core_place, *rest = grid.split(index)
        swapped.append((index, grid.join([core_place, y] + rest)))
    outer_full = lax.all_gather(low(outer_weight), AXES, axis=0, tiled=True)
    outer_full = outer_full.reshape(2, FF // 2, D)
    stages = grid.small_stages()

    owner = grid.small_owner()[:, None]

    def choose_rows(rows, width):
        ids = (owner * rows + jnp.arange(rows, dtype=jnp.int32)[None, :]).reshape(1, -1)
        return low(jnp.arange(width, dtype=jnp.int32)[:, None] == ids)

    choose_attend = choose_rows(attend_rows, 3 * INNER)
    choose_output = choose_rows(output_rows, INNER)

    back_orders = [batch_dims[:0:-1] + [0] + batch_dims[:1], [0] + batch_dims[::-1]]

    def by_row(values):
        return values.reshape(D, row_count, shard_len).transpose(1, 0, 2)

    def by_token(values):
        return values.transpose(1, 0, 2).reshape(D, tokens)

    def to_rows(values):
        width = values.shape[-1]
        return exchange(values.reshape(row_count, shard_len, width)).reshape(LEN, width)

    def to_positions(values):
        width = values.shape[-1]
        return exchange(values.reshape(seq_count, shard_len, width)).reshape(tokens, width)

    own_keep = lax.dynamic_slice_in_dim(keep_mask, seq_place, 1, 0)
    own_rank = jnp.where(own_keep > 0, jnp.cumsum(own_keep, axis=1) - 1, -1)
    own_rank = own_rank.reshape(LEN // QB, QB)

    hidden_in = wide(by_token(hidden.transpose(0, 2, 1)))

    def scale_of(values):
        return lax.rsqrt(jnp.mean(values * values, axis=0, keepdims=True) + EPSILON)

    gains = norm_params[:, :, None]
    scale_one = scale_of(hidden_in)
    normed_one = low(hidden_in * scale_one * gains[0])
    cotangents = spread(own_rank[:, None, :], states_cotangent.reshape(KEEP_CAP, D).T)
    projected = low(mm(normed_one, attend_full, (((0,), (1,)), ((), ()))))
    row_projected = to_rows(projected)
    window = jnp.arange(WB, dtype=jnp.int32)
    offsets = jnp.where(window >= WB - QB, window - WB, window) - (LEN - QB)
    one_hot = wide(
        bucket_of_offset(offsets)[:, None] == jnp.arange(BUCKETS, dtype=jnp.int32)[None, :]
    )
    bias_line = jnp.sum(bias_table[:, None, :] * one_hot[None], axis=-1)
    bias_line = bias_line.reshape(HEADS // 2, 2, WB)
    row_projected, output_full = tie(row_projected, output_full)
    row_mixed, row_lse = attn_fwd(row_projected, bias_line)
    mixed = to_positions(row_mixed)
    cotangents, row_mixed = tie(cotangents, row_mixed)
    mixed, cotangents = tie(mixed, cotangents)
    middle = hidden_in + mm(output_full, mixed, (((0,), (1,)), ((), ())))
    scale_two = scale_of(middle)
    normed_two = low(middle * scale_two * gains[1])
    far_states = grid.shift(normed_two, 1, 1)

    _, inner_full = tie(normed_two, inner_full)
    inner_full, cotangents = tie(inner_full, cotangents)
    cotangents = exchange(cotangents)
    units, slope_gate, slope_up = lift(core, normed_two, far_states, inner_full)
    _, outer_full = tie(units, outer_full)
    units, cotangents = tie(units, cotangents)
    far_part = lower(core, outer_full, units, 1, jnp.bfloat16)
    units, far_part = tie(units, far_part)
    far_part = grid.shift(far_part, 1, 1)
    near_part = lower(core, outer_full, units, 0, jnp.float32)
    state_grad = by_token(cotangents)
    result = middle + near_part + wide(far_part)

    scale_three = scale_of(result)
    gate_line = gains[2] * gains[3]
    gate_dot = jnp.sum(result * gate_line, axis=0, keepdims=True)
    squashed = jax.nn.sigmoid(gate_dot * scale_three)
    keep_local = lax.dynamic_slice_in_dim(keep_mask, seq_place * shard_len, shard_len, 1)
    keep_float = wide(keep_local).reshape(1, tokens)
    kept_gate = (GATE_RANGE * squashed * keep_float).reshape(row_count, shard_len)
    logit_grad = (
        gate_cotangent.reshape(1, tokens) * keep_float * GATE_RANGE * squashed * (1.0 - squashed)
    )
    line_grad = jnp.sum(logit_grad * scale_three * result, axis=1)
    result_grad = (
        wide(state_grad)
        + logit_grad * scale_three * gate_line
        - result * (scale_three * scale_three * scale_three * logit_grad * gate_dot / D)
    )
    result_grad_low = low(result_grad)
    row_result = exchange(by_row(low(result)))
    far_grads = grid.shift(result_grad_low, 1, 1)

    lifted_grad = unlift(core, result_grad_low, far_grads, outer_full, slope_gate, slope_up)
    scatters = []
    for h in range(2):
        if inner_rows % 32 == 0:
            grad = weight_grad(lifted_grad, normed_two, far_states, 4, inner_rows, h)
        else:
            grad = weight_grad(lifted_grad, normed_two, far_states, 8)
            grad = grad.reshape(-1, 2, inner_rows // 2, D)[:, h]
        grad = grad.reshape([2] + batch_sizes + [inner_rows // 2, D])
        scatters.append(Scatter(grid, grad, back_orders[h]))
        lifted_grad = scatters[h].advance(lifted_grad)
    far_part = states_grad(core, inner_full, lifted_grad, 1, jnp.bfloat16)
    lifted_grad, far_part, row_result = tie(lifted_grad, far_part, row_result)
    far_part = grid.shift(far_part, 1, 1)
    near_part = states_grad(core, inner_full, lifted_grad, 0, jnp.float32)
    normed_two_grad = near_part + wide(far_part)
    feed_line = jnp.sum(normed_two_grad * middle * scale_two, axis=1)
    weighted = normed_two_grad * gains[1]
    middle_grad = (
        result_grad
        + scale_two * weighted
        - middle
        * (
            scale_two
            * scale_two
            * scale_two
            * jnp.mean(weighted * middle, axis=0, keepdims=True)
        )
    )
    middle_grad_low = low(middle_grad)

    middle_grad_low = scatters[0].advance(middle_grad_low)
    middle_grad_low = scatters[1].advance(middle_grad_low)
    mixed_grad = low(mm(middle_grad_low, output_full, (((0,), (1,)), ((), ()))))
    units, mixed_grad = tie(units, mixed_grad)
    row_mixed_grad = to_rows(mixed_grad)
    outer_grad = weight_grad(units, result_grad_low, far_grads, 4)
    chosen_mixed = low(mm(mixed, choose_output))
    output_grad = low(mm(chosen_mixed, middle_grad_low, (((0,), (1,)), ((), ()))))
    row_mixed_grad, output_grad, outer_grad = tie(row_mixed_grad, output_grad, outer_grad)
    outer_sum = lax.psum_scatter(outer_grad, ("y", "batch"), scatter_dimension=0, tiled=True)
    row_mixed_grad = scatters[0].advance(row_mixed_grad)
    row_grad, line_sums = attn_bwd(row_projected, row_mixed_grad, row_lse, bias_line)
    inner_sum0 = scatters[0].result(row_grad).reshape(inner_rows // 2, D)
    row_grad, inner_sum0 = tie(row_grad, inner_sum0)
    row_grad = scatters[1].advance(row_grad)
    projected_grad = to_positions(row_grad)
    kept_states = compact(own_rank[:, :, None], row_result).T.reshape(1, 1, KEEP_CAP, D)
    one_hot_rows = jnp.stack([jnp.roll(one_hot, r, axis=0) for r in range(8)])
    table_grad = jnp.einsum(
        "hrw,rwb->hb",
        line_sums.reshape(HEADS, 8, WB),
        one_hot_rows,
        precision=lax.Precision.HIGHEST,
    )
    inner_sum1 = scatters[1].result(table_grad).reshape(inner_rows // 2, D)
    projected_grad, inner_sum1, kept_states, table_grad = tie(
        projected_grad, inner_sum1, kept_states, table_grad
    )
    chosen_grad = low(mm(projected_grad, choose_attend))

    def swap(values, bit):
        pairs = [(index, index ^ bit) for index in range(grid.total)]
        return lax.ppermute(values, AXES, pairs)

    small_grads = [
        low(mm(chosen_grad, normed_one, (((0,), (1,)), ((), ())))),
        output_grad,
    ]
    normed_one_grad = None
    bits = [1 << place for place in range((grid.total - 1).bit_length())]
    for index, (dim, odd_dim) in enumerate(stages[::-1]):
        count = grid.sizes[dim]
        parts = [jnp.split(grad, count, axis=0) for grad in small_grads]
        totals = [wide(part[0]) for part in parts]
        sends = [
            jnp.concatenate([part[step] for part in parts], axis=0) for step in range(1, count)
        ]
        if index > 0:
            if index == 1:
                outer_sum, *sends = tie(outer_sum, *sends)
            lines, *sends = tie(lines, *sends)
            lines = lines + swap(lines, bits.pop(0))
        moved = [grid.shift(send, dim, -step - 1, odd_dim) for step, send in enumerate(sends)]
        if index == 0:
            normed_one_grad = mm(attend_full, projected_grad, (((0,), (1,)), ((), ())))
            attend_line = jnp.sum(normed_one_grad * hidden_in * scale_one, axis=1)
            lines = jnp.stack(
                [
                    attend_line,
                    feed_line,
                    line_grad * norm_params[3],
                    line_grad * norm_params[2],
                    jnp.pad(table_grad.reshape(-1), (0, D - HEADS * BUCKETS)),
                ]
            )
        rows = totals[0].shape[0]
        for part in moved:
            totals = [totals[0] + wide(part[:rows]), totals[1] + wide(part[rows:])]
        small_grads = [low(total) for total in totals]
    while bits:
        lines = lines + swap(lines, bits.pop(0))
    weighted_one = normed_one_grad * gains[0]
    input_grad = low(
        middle_grad
        + scale_one * weighted_one
        - hidden_in
        * (
            scale_one
            * scale_one
            * scale_one
            * jnp.mean(weighted_one * hidden_in, axis=0, keepdims=True)
        )
    )
    input_grad = by_row(input_grad).transpose(0, 2, 1)

    inner_sum = jnp.concatenate([inner_sum0, inner_sum1], axis=0).T
    outer_sum = wide(lax.ppermute(outer_sum, AXES, swapped))
    attend_sum = totals[0].T
    output_sum = totals[1]
    norm_total = lines[:4]
    table_total = lines[4, : HEADS * BUCKETS].reshape(HEADS, BUCKETS)

    steps_done = wide(step_count[0])
    bias_one = 1.0 - MOMENT_DECAY**steps_done
    bias_two = 1.0 - SQUARE_DECAY**steps_done
    smooth_decay = (1.0 + steps_done) / (10.0 + steps_done)

    def updated(weight, first, second, grad, rate, average):
        return adam_step(
            weight, first, second, grad, rate, bias_one, bias_two, average, smooth_decay
        )

    return (
        kept_states,
        kept_gate,
        input_grad,
        *updated(
            attend_weight, attend_first, attend_second, attend_sum, RATE_ATTEND, attend_average
        ),
        *updated(
            output_weight, output_first, output_second, output_sum, RATE_OUTPUT, output_average
        ),
        *updated(inner_weight, inner_first, inner_second, inner_sum, RATE_INNER, inner_average),
        *updated(outer_weight, outer_first, outer_second, outer_sum, RATE_OUTER, outer_average),
        *updated(norm_params, norm_first, norm_second, norm_total, RATE_NORM, norm_average),
        *updated(bias_table, table_first, table_second, table_total, RATE_TABLE, table_average),
    )


def solution(mesh):
    placed = (
        P("batch", ("y", "core"), None),
        P("batch", None),
        P("batch", ("y", "core"), None, None),
        P("batch", ("y", "core")),
        P(),
        P(None, ("y", "core", "batch")),
        P(None, ("y", "core", "batch")),
        P(None, ("y", "core", "batch")),
        P(None, ("y", "core", "batch")),
        P(("y", "core", "batch"), None),
        P(("y", "core", "batch"), None),
        P(("y", "core", "batch"), None),
        P(("y", "core", "batch"), None),
        P(None, ("y", "core", "batch")),
        P(None, ("y", "core", "batch")),
        P(None, ("y", "core", "batch")),
        P(None, ("y", "core", "batch")),
        P(("y", "core", "batch"), None),
        P(("y", "core", "batch"), None),
        P(("y", "core", "batch"), None),
        P(("y", "core", "batch"), None),
        P(),
        P(),
        P(),
        P(),
        P(),
        P(),
        P(),
        P(),
    )
    devices = mesh.devices.reshape(mesh.shape["seq"] // 2, 2, mesh.shape["batch"])
    finer = jax.sharding.Mesh(devices, ("y", "core", "batch"))
    return jax.shard_map(
        functools.partial(per_device, mesh.shape["seq"], mesh.shape["batch"]),
        mesh=finer,
        in_specs=placed,
        out_specs=(
            P("batch", ("y", "core"), None, None),
            P("batch", ("y", "core")),
            P("batch", ("y", "core"), None),
            P(None, ("y", "core", "batch")),
            P(None, ("y", "core", "batch")),
            P(None, ("y", "core", "batch")),
            P(None, ("y", "core", "batch")),
            P(("y", "core", "batch"), None),
            P(("y", "core", "batch"), None),
            P(("y", "core", "batch"), None),
            P(("y", "core", "batch"), None),
            P(None, ("y", "core", "batch")),
            P(None, ("y", "core", "batch")),
            P(None, ("y", "core", "batch")),
            P(None, ("y", "core", "batch")),
            P(("y", "core", "batch"), None),
            P(("y", "core", "batch"), None),
            P(("y", "core", "batch"), None),
            P(("y", "core", "batch"), None),
            P(),
            P(),
            P(),
            P(),
            P(),
            P(),
            P(),
            P(),
        ),
        check_vma=False,
    )
```

```python
import functools

import jax
import jax.numpy as jnp
from jax import lax
from jax.experimental import pallas as pl
from jax.experimental.pallas import tpu as pltpu
from jax.sharding import PartitionSpec as P

D = 1472
HEADS = 6
HEAD_DIM = 64
FF = 3584
BUCKETS = 32
LEN = 1024
INNER = 384
KEEP_CAP = 768


EPSILON = 1e-06
GATE_RANGE = -30.0
MOMENT_DECAY = 0.9
SQUARE_DECAY = 0.999
ADAM_FLOOR = 1e-08
WEIGHT_DECAY = 0.01
RATE_ATTEND = 0.02
RATE_OUTPUT = 4.0
RATE_INNER = 0.06
RATE_OUTER = 0.04
RATE_NORM = 0.5
RATE_TABLE = 1.0
far_edges = (12, 16, 23, 32, 46, 64, 91)
AXES = ("y", "core", "batch")
FREE = pl.CostEstimate(flops=0, bytes_accessed=0, transcendentals=0)
QB = 256
WB = 2048
MIB = 2**20
NT = (((1,), (1,)), ((), ()))
TN = (((0,), (0,)), ((), ()))


def cost(micros):
    return pl.CostEstimate(flops=micros * 10**9, bytes_accessed=0, transcendentals=0)


def mm(a,b,dims=(((1,),(0,)),((),()))):
    return lax.dot_general(a,b,dims,preferred_element_type=jnp.float32)
def head_mask(shape,h):
    lane=lax.broadcasted_iota(jnp.int32,shape,1)
    return (lane<64) if h==0 else (lane>=64)
def fill_bias(t_ref,b_ref):
    for h in range(2):
        row=jnp.broadcast_to(t_ref[0,h:h+1,:],(QB,WB))
        b_ref[h]=pltpu.roll(row,0,1,stride=1,stride_axis=0)
def fwd_kernel(q_ref,k_ref,v_ref,t_ref,o_ref,l_ref,b_ref):
    fill_bias(t_ref,b_ref)
    k=k_ref[...]; v=v_ref[...]
    nq=LEN//QB
    def body(i,_):
        rows=pl.ds(pl.multiple_of(i*QB,QB),QB)
        qb=q_ref[rows,:]
        cols=pl.ds(pl.multiple_of((nq-1-i)*QB,QB),LEN)
        outs=[];ls=[]
        for h in range(2):
            qm=jnp.where(head_mask(qb.shape,h),qb,jnp.zeros_like(qb))
            s=mm(qm,k,NT)+b_ref[h,:,cols]
            m=jnp.max(s,-1,keepdims=True)
            e=jnp.exp(s-m)
            l=jnp.sum(e,-1,keepdims=True)
            o=mm((e*(1.0/l)).astype(jnp.bfloat16),v)
            outs.append(o); ls.append(m+jnp.log(l))
        msk=head_mask(outs[0].shape,0)
        o_ref[rows,:]=jnp.where(msk,outs[0],outs[1]).astype(o_ref.dtype)
        l_ref[rows,:]=jnp.where(msk,jnp.broadcast_to(ls[0],outs[0].shape),jnp.broadcast_to(ls[1],outs[0].shape))
        return 0
    lax.fori_loop(0,nq,body,0)
def attn_fwd(qkv,tvec):
    n=INNER//128
    return pl.pallas_call(fwd_kernel,grid=(n,),
        in_specs=[pl.BlockSpec((LEN,128),lambda h:(0,h)),pl.BlockSpec((LEN,128),lambda h:(0,n+h)),pl.BlockSpec((LEN,128),lambda h:(0,2*n+h)),
                  pl.BlockSpec((1,2,WB),lambda h:(h,0,0))],
        out_specs=[pl.BlockSpec((LEN,128),lambda h:(0,h)),pl.BlockSpec((LEN,128),lambda h:(0,h))],
        out_shape=[jax.ShapeDtypeStruct((LEN,INNER),jnp.bfloat16),jax.ShapeDtypeStruct((LEN,INNER),jnp.float32)],
        scratch_shapes=[pltpu.VMEM((2,QB,WB),jnp.float32)],
        compiler_params=pltpu.CompilerParams(vmem_limit_bytes=48*2**20),
        cost_estimate=cost(3),
        name="attn_fwd")(qkv,qkv,qkv,tvec)
def bwd_kernel(q_ref,k_ref,v_ref,g_ref,l_ref,t_ref,o_ref,dt_ref,b_ref,db_ref,dk_ref,dv_ref):
    fill_bias(t_ref,b_ref)
    db_ref[...]=jnp.zeros_like(db_ref)
    dk_ref[...]=jnp.zeros_like(dk_ref)
    dv_ref[...]=jnp.zeros_like(dv_ref)
    k=k_ref[...]; v=v_ref[...]
    nq=LEN//QB
    hp=pl.program_id(0)
    def body(i,_):
        rows=pl.ds(pl.multiple_of(i*QB,QB),QB)
        qb=q_ref[rows,:]; gb=g_ref[rows,:]; lb=l_ref[rows,:]
        cols=pl.ds(pl.multiple_of((nq-1-i)*QB,QB),LEN)
        dqs=[]
        for h in range(2):
            hm=head_mask(qb.shape,h)
            qm=jnp.where(hm,qb,jnp.zeros_like(qb)); gm=jnp.where(hm,gb,jnp.zeros_like(gb))
            s=mm(qm,k,NT)+b_ref[h,:,cols]
            p=jnp.exp(s-lb[:,64*h:64*h+1])
            dp=mm(gm,v,NT)
            t=p*dp
            d=jnp.sum(t,-1,keepdims=True)
            ds=(t-p*d)
            db_ref[h,:,cols]+=ds
            ds=ds.astype(jnp.bfloat16)
            dv_ref[...]+=mm(p.astype(jnp.bfloat16),gm,TN)
            dk_ref[...]+=mm(ds,qm,TN)
            dqs.append(mm(ds,k))
        o_ref[rows,pl.ds(pl.multiple_of(hp*128,128),128)]=jnp.where(head_mask(dqs[0].shape,0),dqs[0],dqs[1]).astype(o_ref.dtype)
        return 0
    lax.fori_loop(0,nq,body,0)
    o_ref[:,pl.ds(pl.multiple_of(INNER+hp*128,128),128)]=dk_ref[...].astype(o_ref.dtype)
    o_ref[:,pl.ds(pl.multiple_of(2*INNER+hp*128,128),128)]=dv_ref[...].astype(o_ref.dtype)
    for h in range(2):
        rows=QB//2
        while rows>=8:
            db_ref[h,:rows,:]=db_ref[h,:rows,:]+pltpu.roll(db_ref[h,rows:2*rows,:],WB-rows,1)
            rows//=2
        dt_ref[0,h]=db_ref[h,:8,:]
def attn_bwd(qkv,grad,lse,tvec):
    n=INNER//128
    return pl.pallas_call(bwd_kernel,grid=(n,),
        in_specs=[pl.BlockSpec((LEN,128),lambda h:(0,h)),pl.BlockSpec((LEN,128),lambda h:(0,n+h)),pl.BlockSpec((LEN,128),lambda h:(0,2*n+h)),
                  pl.BlockSpec((LEN,128),lambda h:(0,h)),pl.BlockSpec((LEN,128),lambda h:(0,h)),
                  pl.BlockSpec((1,2,WB),lambda h:(h,0,0))],
        out_specs=[pl.BlockSpec((LEN,3*INNER),lambda h:(0,0)),pl.BlockSpec((1,2,8,WB),lambda h:(h,0,0,0))],
        out_shape=[jax.ShapeDtypeStruct((LEN,3*INNER),jnp.bfloat16),jax.ShapeDtypeStruct((n,2,8,WB),jnp.float32)],
        scratch_shapes=[pltpu.VMEM((2,QB,WB),jnp.float32),pltpu.VMEM((2,QB,WB),jnp.float32),pltpu.VMEM((LEN,128),jnp.float32),pltpu.VMEM((LEN,128),jnp.float32)],
        compiler_params=pltpu.CompilerParams(vmem_limit_bytes=48*2**20),
        cost_estimate=cost(5),
        name="attn_bwd")(qkv,qkv,qkv,grad,lse,tvec)


def bucket_of_offset(offset):
    distance = jnp.abs(offset)
    far_bucket = jnp.full(distance.shape, 8, jnp.int32)
    for edge_value in far_edges:
        far_bucket = far_bucket + (distance >= edge_value).astype(jnp.int32)
    near_bucket = jnp.where(distance < 8, distance, far_bucket)
    return near_bucket + jnp.where(offset > 0, 16, 0)


def adam_step(weight, first, second, grad, rate, bias_one, bias_two, average, smooth_decay):
    first_new = MOMENT_DECAY * first + (1.0 - MOMENT_DECAY) * grad
    second_new = SQUARE_DECAY * second + (1.0 - SQUARE_DECAY) * grad * grad
    direction = first_new / bias_one / (jnp.sqrt(second_new / bias_two) + ADAM_FLOOR)
    weight_new = weight - rate * (direction + WEIGHT_DECAY * weight)
    average_new = smooth_decay * average + (1.0 - smooth_decay) * weight_new
    return (weight_new, first_new, second_new, average_new)


def low(values):
    return values.astype(jnp.bfloat16)


def wide(values):
    return values.astype(jnp.float32)


def tie(*values):
    return lax.optimization_barrier(values)


class Grid:
    def __init__(self, seq_count, batch_count):
        if batch_count == 8:
            digits = [4, 2]
        else:
            digits, rest = [], batch_count
            while rest % 4 == 0:
                digits, rest = [4] + digits, rest // 4
            if rest > 1:
                digits = [rest] + digits
        self.sizes = [seq_count // 2, 2] + digits
        self.total = seq_count * batch_count
        self.batch_dims = list(range(2, len(self.sizes)))
        self.swaps = self.sizes[-1] == self.sizes[0]

    def split(self, index):
        out = []
        for size in reversed(self.sizes):
            out.append(index % size)
            index = index // size
        return out[::-1]

    def join(self, coords):
        index = 0
        for size, coord in zip(self.sizes, coords):
            index = index * size + coord
        return index

    def shift(self, values, dim, step, odd_dim=None):
        pairs = []
        for index in range(self.total):
            coords = self.split(index)
            along = dim if odd_dim is None or coords[1] == 0 else odd_dim
            coords[along] = (coords[along] + step) % self.sizes[along]
            pairs.append((index, self.join(coords)))
        return lax.ppermute(values, AXES, pairs)

    def mine(self):
        return self.split(lax.axis_index(AXES))

    def small_stages(self):
        first = [(dim, dim) for dim in self.batch_dims[:-1]]
        x, y = self.batch_dims[-1], 0
        if self.swaps:
            return first + [(x, y), (y, x), (1, 1)]
        return first + [(x, x), (y, y), (1, 1)]

    def small_owner(self):
        stages = self.small_stages()
        rest = jnp.arange(self.total, dtype=jnp.int32)
        steps = []
        for dim, _ in stages:
            steps.append(rest % self.sizes[dim])
            rest = rest // self.sizes[dim]
        mine = self.mine()
        core = (mine[1] + steps[-1]) % 2
        coords = list(mine)
        coords[1] = core
        for (dim, odd_dim), step in zip(stages[:-1], steps[:-1]):
            if dim == odd_dim:
                coords[dim] = (coords[dim] - step) % self.sizes[dim]
            else:
                for this, other in ((dim, 0), (odd_dim, 1)):
                    coords[this] = jnp.where(
                        core == other, (coords[this] - step) % self.sizes[this], coords[this]
                    )
        return self.join(coords)


def absolute(parts, place):
    count = len(parts)
    if count == 2:
        first = place == 0
        return [jnp.where(first, parts[0], parts[1]), jnp.where(first, parts[1], parts[0])]
    return [
        lax.select_n(lax.rem(place - j + count, count), *parts) for j in range(count)
    ]


class Gather:
    def __init__(self, grid, piece, order):
        self.grid = grid
        self.plan = list(order)
        self.parts = [piece]

    def close(self):
        dim = self.plan.pop(0)
        place = self.grid.mine()[dim]
        axis = max(dim - 1, 0)
        if len(self.parts) == 2:
            self.parts = [jnp.concatenate(absolute(self.parts, place), axis=axis)]
            return
        count = len(self.parts)
        whole = jnp.concatenate(self.parts, axis=axis)
        for j, part in enumerate(self.parts):
            whole = lax.dynamic_update_slice_in_dim(
                whole, part, lax.rem(place - j + count, count), axis
            )
        self.parts = [whole]

    def send(self):
        dim = self.plan[0]
        for step in range(1, self.grid.sizes[dim]):
            self.parts.append(self.grid.shift(self.parts[0], dim, step))

    def advance(self, *values):
        if len(self.parts) > 1:
            _, *self.parts = tie(values[0], *self.parts)
            self.close()
        if self.plan:
            *values, self.parts[0] = tie(*values, self.parts[0])
            self.send()
        return values[0] if len(values) == 1 else values

    def result(self, value):
        if len(self.parts) > 1:
            _, *self.parts = tie(value, *self.parts)
        while self.plan:
            if len(self.parts) > 1:
                self.close()
            if self.plan:
                self.send()
        return self.parts[0]


class Scatter:
    def __init__(self, grid, pieces, order):
        self.grid = grid
        self.plan = list(order)
        self.sent = False
        self.start(pieces)

    def start(self, pieces):
        dim = self.plan[0]
        count = self.grid.sizes[dim]
        axis = max(dim - 1, 0)
        place = self.grid.mine()[dim]
        if count == 2:
            parts = [lax.slice_in_dim(pieces, j, j + 1, axis=axis) for j in range(count)]
            self.parts = absolute(parts, place)
        else:
            self.parts = [
                lax.dynamic_slice_in_dim(pieces, lax.rem(place - j + count, count), 1, axis)
                for j in range(count)
            ]

    def settle(self):
        self.plan.pop(0)
        total = wide(self.parts[0])
        for part in self.parts[1:]:
            total = total + wide(part)
        self.total = low(total) if self.plan else total
        self.sent = False
        if self.plan:
            self.start(self.total)

    def send(self):
        dim = self.plan[0]
        for step in range(1, len(self.parts)):
            self.parts[step] = self.grid.shift(self.parts[step], dim, -step)
        self.sent = True

    def advance(self, *values):
        if self.sent:
            _, *self.parts = tie(values[0], *self.parts)
            self.settle()
        if self.plan:
            count = len(self.parts) - 1
            tied = tie(*values, *self.parts[1:])
            self.parts[1:] = tied[-count:]
            values = tied[:-count]
            self.send()
        return values[0] if len(values) == 1 else values

    def result(self, value):
        if self.sent:
            _, *self.parts = tie(value, *self.parts)
        while self.plan:
            if self.sent:
                self.settle()
            if self.plan:
                self.send()
        return self.total


def exchange(values):
    return lax.all_to_all(values, ("y", "core"), split_axis=0, concat_axis=0, tiled=True)


def pick(near_ref, far_ref):
    step = pl.program_id(0)
    return jnp.where(step < pl.num_programs(0) // 2, near_ref[...], far_ref[...])


def pair_specs(rows, blocks):
    return [
        pl.BlockSpec((rows, QB), lambda t, core: (0, jnp.minimum(t, blocks - 1))),
        pl.BlockSpec((rows, QB), lambda t, core: (0, jnp.maximum(t - blocks, 0))),
    ]


def by_core(kernel, grid, in_specs, out_specs, out_shape, name, micros):
    return pl.pallas_call(
        lambda core_ref, *refs: kernel(*refs),
        grid_spec=pltpu.PrefetchScalarGridSpec(
            num_scalar_prefetch=1, grid=grid, in_specs=in_specs, out_specs=out_specs
        ),
        out_shape=out_shape,
        compiler_params=pltpu.CompilerParams(vmem_limit_bytes=56 * MIB),
        cost_estimate=cost(micros),
        name=name,
    )


def weight_spec(first):
    return pl.BlockSpec((1, FF // 2, D), lambda t, core: (first + core[0], 0, 0))


def own_spec():
    return pl.BlockSpec((1, FF // 2, D), lambda t, core: (0, 0, 0))


def token_spec(rows, first=0):
    return pl.BlockSpec((rows, QB), lambda t, core: (0, first + t))


def lift_kernel(near_ref, far_ref, g_ref, u_ref, units_ref, da_ref, db_ref):
    block = pick(near_ref, far_ref)
    rows = units_ref.shape[0] // 2
    for part in range(2):
        here = slice(part * rows, (part + 1) * rows)
        gate = mm(g_ref[0, here, :], block)
        up = mm(u_ref[0, here, :], block)
        root = 0.7978845608028654
        square = gate * gate
        inside = jnp.tanh(root * gate * (1.0 + 0.044715 * square))
        half = 0.5 * (1.0 + inside)
        active = gate * half
        slope = half + 0.5 * gate * (1.0 - inside * inside) * (
            root * (1.0 + 3.0 * 0.044715 * square)
        )
        units_ref[here, :] = low(active * up)
        da_ref[here, :] = low(up * slope)
        db_ref[here, :] = low(active)


def lift(core, near, far, inner_full):
    tokens = 2 * near.shape[1]
    blocks = near.shape[1] // QB
    out = jax.ShapeDtypeStruct((FF // 2, tokens), jnp.bfloat16)
    return by_core(
        lift_kernel,
        (2 * blocks,),
        pair_specs(D, blocks) + [weight_spec(0), weight_spec(2)],
        [token_spec(FF // 2)] * 3,
        [out] * 3,
        "lift",
        5,
    )(core, near, far, inner_full, inner_full)


def unlift_kernel(near_ref, far_ref, w_ref, da_ref, db_ref, out_ref):
    half = w_ref.shape[1]
    units_grad = mm(w_ref[0], pick(near_ref, far_ref))
    out_ref[:half, :] = low(units_grad * wide(da_ref[...]))
    out_ref[half:, :] = low(units_grad * wide(db_ref[...]))


def unlift(core, near, far, outer_full, slope_gate, slope_up):
    tokens = 2 * near.shape[1]
    blocks = near.shape[1] // QB
    return by_core(
        unlift_kernel,
        (2 * blocks,),
        pair_specs(D, blocks) + [own_spec()] + [token_spec(FF // 2)] * 2,
        token_spec(FF),
        jax.ShapeDtypeStruct((FF, tokens), jnp.bfloat16),
        "unlift",
        3,
    )(core, near, far, outer_full, slope_gate, slope_up)


def lower_kernel(w_ref, units_ref, out_ref):
    out_ref[...] = mm(w_ref[0], units_ref[...], TN).astype(out_ref.dtype)


def lower(core, outer_full, units, first, dtype):
    tokens = units.shape[1] // 2
    return by_core(
        lower_kernel,
        (tokens // QB,),
        [own_spec(), token_spec(FF // 2, first * (tokens // QB))],
        token_spec(D),
        jax.ShapeDtypeStruct((D, tokens), dtype),
        "lower",
        2,
    )(core, outer_full, units)


def states_grad_kernel(g_ref, u_ref, grad_ref, out_ref):
    half = g_ref.shape[1]
    total = mm(g_ref[0], grad_ref[:half, :], TN)
    out_ref[...] = (total + mm(u_ref[0], grad_ref[half:, :], TN)).astype(out_ref.dtype)


def states_grad(core, inner_full, lifted_grad, first, dtype):
    tokens = lifted_grad.shape[1] // 2
    return by_core(
        states_grad_kernel,
        (tokens // QB,),
        [weight_spec(0), weight_spec(2), token_spec(FF, first * (tokens // QB))],
        token_spec(D),
        jax.ShapeDtypeStruct((D, tokens), dtype),
        "states_grad",
        0,
    )(core, inner_full, inner_full, lifted_grad)


def whole(shape):
    return pl.BlockSpec(shape, lambda *_: (0,) * len(shape))


def weight_grad_kernel(block, half, left_ref, near_ref, far_ref, out_ref):
    tokens = near_ref.shape[1]
    left = left_ref[...]
    if half is not None:
        starts = range(half * (block // 2), left.shape[0], block)
        left = jnp.concatenate([left[start : start + block // 2] for start in starts], axis=0)
    total = mm(left[:, :tokens], near_ref[...], NT)
    out_ref[...] = low(total + mm(left[:, tokens:], far_ref[...], NT))


def weight_grad(left, near, far, count, block=None, half=None):
    tokens = near.shape[1]
    tile = left.shape[0] // count
    rows = tile if half is None else tile // 2
    return pl.pallas_call(
        functools.partial(weight_grad_kernel, block, half),
        grid=(count,),
        in_specs=[
            pl.BlockSpec((tile, 2 * tokens), lambda f: (f, 0)),
            whole((D, tokens)),
            whole((D, tokens)),
        ],
        out_specs=pl.BlockSpec((rows, D), lambda f: (f, 0)),
        out_shape=jax.ShapeDtypeStruct((count * rows, D), jnp.bfloat16),
        compiler_params=pltpu.CompilerParams(vmem_limit_bytes=56 * MIB),
        cost_estimate=cost(2),
        name="weight_grad",
    )(left, near, far)


def scale_of(values):
    return lax.rsqrt(jnp.mean(values * values, axis=0, keepdims=True) + EPSILON)


def add_line(line_ref, values):
    total = jnp.sum(values, axis=1, keepdims=True)

    @pl.when(pl.program_id(0) == 0)
    def _():
        line_ref[...] = total

    @pl.when(pl.program_id(0) > 0)
    def _():
        line_ref[...] += total


def back_through_norm(values, scale, weighted):
    inner_mean = jnp.mean(weighted * values, axis=0, keepdims=True)
    return scale * weighted - values * (scale * scale * scale * inner_mean)


def gate_kernel(
    middle_ref, near_ref, far_ref, state_ref, cot_ref, keep_ref, gain_ref,
    result_ref, grad_ref, low_ref, gate_ref, line_ref,
):
    result = middle_ref[...] + near_ref[...] + wide(far_ref[...])
    result_ref[0] = low(result)
    scale = scale_of(result)
    gain = gain_ref[...]
    dot = jnp.sum(result * gain, axis=0, keepdims=True)
    squashed = jax.nn.sigmoid(dot * scale)
    keep = keep_ref[0]
    gate_ref[0] = GATE_RANGE * squashed * keep
    logit_grad = cot_ref[0] * keep * GATE_RANGE * squashed * (1.0 - squashed)
    share = logit_grad * scale
    grad = (
        wide(state_ref[0]) + share * gain - result * (share * scale * scale * dot * (1.0 / D))
    )
    grad_ref[...] = grad
    low_ref[...] = low(grad)
    add_line(line_ref, share * result)


def mid_kernel(near_ref, far_ref, middle_ref, grad_ref, gain_ref, out_ref, low_ref, line_ref):
    normed_grad = near_ref[...] + wide(far_ref[...])
    middle = middle_ref[...]
    scale = scale_of(middle)
    total = grad_ref[...] + back_through_norm(middle, scale, normed_grad * gain_ref[...])
    out_ref[...] = total
    low_ref[...] = low(total)
    add_line(line_ref, normed_grad * middle * scale)


def last_kernel(w_ref, projected_ref, hidden_ref, grad_ref, gain_ref, out_ref, line_ref):
    normed_grad = mm(w_ref[...], projected_ref[...], (((0,), (1,)), ((), ())))
    hidden = wide(hidden_ref[0])
    scale = scale_of(hidden)
    out_ref[0] = low(
        grad_ref[...] + back_through_norm(hidden, scale, normed_grad * gain_ref[...])
    )
    add_line(line_ref, normed_grad * hidden * scale)


WIDE = pl.BlockSpec((D, QB), lambda t: (0, t))
ROW = pl.BlockSpec((1, D, QB), lambda t: (t, 0, 0))
THIN = pl.BlockSpec((1, 1, QB), lambda t: (t, 0, 0))
COLUMN = pl.BlockSpec((D, 1), lambda t: (0, 0))
COLUMN_SHAPE = jax.ShapeDtypeStruct((D, 1), jnp.float32)


def over_blocks(kernel, count, in_specs, out_specs, out_shape, name):
    return pl.pallas_call(
        kernel,
        grid=(count,),
        in_specs=in_specs,
        out_specs=out_specs,
        out_shape=out_shape,
        compiler_params=pltpu.CompilerParams(vmem_limit_bytes=56 * MIB),
        cost_estimate=cost(0),
        name=name,
    )


def spread_kernel(rank_ref, cot_ref, out_ref):
    slot = lax.broadcasted_iota(jnp.int32, (KEEP_CAP, QB), 0)
    chosen = low(jnp.where(slot == rank_ref[0], 1.0, 0.0))
    out_ref[0] = low(mm(cot_ref[...], chosen))


def spread(rank, cotangent):
    blocks = rank.shape[0]
    return pl.pallas_call(
        spread_kernel,
        grid=(blocks,),
        in_specs=[
            pl.BlockSpec((1, 1, QB), lambda i: (i, 0, 0)),
            pl.BlockSpec((D, KEEP_CAP), lambda i: (0, 0)),
        ],
        out_specs=pl.BlockSpec((1, D, QB), lambda i: (i, 0, 0)),
        out_shape=jax.ShapeDtypeStruct((blocks, D, QB), jnp.bfloat16),
        compiler_params=pltpu.CompilerParams(vmem_limit_bytes=40 * MIB),
        cost_estimate=cost(1),
        name="spread",
    )(rank, cotangent)


def compact_kernel(rank_ref, rows_ref, out_ref, sum_ref):
    slot = lax.broadcasted_iota(jnp.int32, (QB, KEEP_CAP), 1)
    chosen = low(jnp.where(slot == rank_ref[0], 1.0, 0.0))
    part = mm(rows_ref[0], chosen)

    @pl.when(pl.program_id(0) == 0)
    def _():
        sum_ref[...] = part

    @pl.when(pl.program_id(0) > 0)
    def _():
        sum_ref[...] += part

    @pl.when(pl.program_id(0) == pl.num_programs(0) - 1)
    def _():
        out_ref[...] = low(sum_ref[...])


def compact(rank, rows):
    blocks = rank.shape[0]
    return pl.pallas_call(
        compact_kernel,
        grid=(blocks,),
        in_specs=[
            pl.BlockSpec((1, QB, 1), lambda i: (i, 0, 0)),
            pl.BlockSpec((1, D, QB), lambda i: (i, 0, 0)),
        ],
        out_specs=pl.BlockSpec((D, KEEP_CAP), lambda i: (0, 0)),
        out_shape=jax.ShapeDtypeStruct((D, KEEP_CAP), jnp.bfloat16),
        scratch_shapes=[pltpu.VMEM((D, KEEP_CAP), jnp.float32)],
        compiler_params=pltpu.CompilerParams(vmem_limit_bytes=40 * MIB),
        cost_estimate=cost(1),
        name="compact",
    )(rank, rows)


def per_device(
    seq_count,
    batch_count,
    hidden,
    keep_mask,
    states_cotangent,
    gate_cotangent,
    step_count,
    attend_weight,
    attend_first,
    attend_second,
    attend_average,
    output_weight,
    output_first,
    output_second,
    output_average,
    inner_weight,
    inner_first,
    inner_second,
    inner_average,
    outer_weight,
    outer_first,
    outer_second,
    outer_average,
    norm_params,
    norm_first,
    norm_second,
    norm_average,
    bias_table,
    table_first,
    table_second,
    table_average,
):
    grid = Grid(seq_count, batch_count)
    batch_dims = grid.batch_dims
    batch_sizes = [grid.sizes[dim] for dim in batch_dims]
    ones = (1,) * len(batch_dims)
    seq_place = lax.axis_index(("y", "core"))
    row_count, shard_len = hidden.shape[0], hidden.shape[1]
    tokens = row_count * shard_len
    attend_rows, output_rows = attend_weight.shape[1], output_weight.shape[0]
    inner_rows, outer_rows = inner_weight.shape[1], outer_weight.shape[0]
    half_ff = FF // 2

    core = lax.axis_index("core").reshape(1).astype(jnp.int32)
    small_rows = attend_rows + output_rows
    small = jnp.concatenate([low(attend_weight).T, low(output_weight)], axis=0)[None]
    stages = grid.small_stages()

    def small_stage(blocks, stage):
        dim, odd_dim = stage
        parts = [blocks] + [
            grid.shift(blocks, dim, step, odd_dim) for step in range(1, grid.sizes[dim])
        ]
        return jnp.concatenate(parts, axis=0)

    swapped = []
    for index in range(grid.total):
        y, core_place, *rest = grid.split(index)
        swapped.append((index, grid.join([core_place, y] + rest)))
    small = small_stage(small, stages[0])
    outer_piece = lax.ppermute(low(outer_weight), AXES, swapped)
    inner_piece = low(inner_weight).T
    hidden, inner_piece = tie(hidden, inner_piece)
    owner = grid.small_owner()[:, None]

    def choose_rows(rows, width):
        ids = (owner * rows + jnp.arange(rows, dtype=jnp.int32)[None, :]).reshape(1, -1)
        return low(jnp.arange(width, dtype=jnp.int32)[:, None] == ids)

    ids = jnp.arange(small_rows, dtype=jnp.int32)[None, :]
    place = jnp.where(
        ids < attend_rows,
        owner * attend_rows + ids,
        3 * INNER + owner * output_rows + ids - attend_rows,
    ).reshape(1, -1)
    choose = low(jnp.arange(4 * INNER, dtype=jnp.int32)[:, None] == place)
    choose_attend = choose_rows(attend_rows, 3 * INNER)
    choose_output = choose_rows(output_rows, INNER)
    choose_attend, choose_output = tie(choose_attend, choose_output)

    back_orders = [batch_dims[:0:-1] + [0] + batch_dims[:1], [0] + batch_dims[::-1]]

    def by_token(values):
        return values.transpose(1, 0, 2).reshape(D, tokens)

    def to_rows(values):
        width = values.shape[-1]
        return exchange(values.reshape(row_count, shard_len, width)).reshape(LEN, width)

    def to_positions(values):
        width = values.shape[-1]
        return exchange(values.reshape(seq_count, shard_len, width)).reshape(tokens, width)

    own_keep = lax.dynamic_slice_in_dim(keep_mask, seq_place, 1, 0)
    own_rank = jnp.where(own_keep > 0, jnp.cumsum(own_keep, axis=1) - 1, -1)
    own_rank = own_rank.reshape(LEN // QB, QB)

    hidden_in = wide(by_token(hidden.transpose(0, 2, 1)))

    gains = norm_params[:, :, None]
    scale_one = scale_of(hidden_in)
    normed_one = low(hidden_in * scale_one * gains[0])
    cotangents = spread(own_rank[:, None, :], states_cotangent.reshape(KEEP_CAP, D).T)
    small, normed_one = tie(small, normed_one)
    for stage in stages[1:-1]:
        small = small_stage(small, stage)
    small, inner_piece, outer_piece = tie(small, inner_piece, outer_piece)
    inner_full = lax.all_gather(inner_piece, AXES, axis=0, tiled=True)
    inner_full = inner_full.reshape(4, FF // 2, D)
    small = small_stage(small, stages[-1]).reshape(grid.total * small_rows, D)
    outer_piece = outer_piece.reshape((1,) + ones + (outer_rows, D))
    gather = Gather(grid, outer_piece, batch_dims + [0])
    gather.send()
    attend_full = low(mm(choose[: 3 * INNER], small))
    projected = low(mm(normed_one, attend_full, (((0,), (1,)), ((), ()))))
    _, small = tie(projected, small)
    output_full = low(mm(choose[3 * INNER :], small))
    row_projected = to_rows(projected)
    window = jnp.arange(WB, dtype=jnp.int32)
    offsets = jnp.where(window >= WB - QB, window - WB, window) - (LEN - QB)
    one_hot = wide(
        bucket_of_offset(offsets)[:, None] == jnp.arange(BUCKETS, dtype=jnp.int32)[None, :]
    )
    bias_line = jnp.sum(bias_table[:, None, :] * one_hot[None], axis=-1)
    bias_line = bias_line.reshape(HEADS // 2, 2, WB)
    output_full = gather.advance(output_full)
    row_projected, output_full = tie(row_projected, output_full)
    row_mixed, row_lse = attn_fwd(row_projected, bias_line)
    mixed = to_positions(row_mixed)
    mixed, cotangents = tie(mixed, cotangents)
    mixed = gather.advance(mixed)
    cotangents, row_mixed = tie(cotangents, row_mixed)
    mixed, cotangents = tie(mixed, cotangents)
    middle = hidden_in + mm(output_full, mixed, (((0,), (1,)), ((), ())))
    scale_two = scale_of(middle)
    normed_two = low(middle * scale_two * gains[1])
    far_states = grid.shift(normed_two, 1, 1)

    _, inner_full = tie(normed_two, inner_full)
    inner_full, cotangents = tie(inner_full, cotangents)
    cotangents = exchange(cotangents)
    units, slope_gate, slope_up = lift(core, normed_two, far_states, inner_full)
    outer_full = gather.result(units).reshape(1, FF // 2, D)
    far_part = lower(core, outer_full, units, 1, jnp.bfloat16)
    units, far_part, cotangents = tie(units, far_part, cotangents)
    near_part = lower(core, outer_full, units, 0, jnp.float32)

    blocks = tokens // QB
    keep_local = lax.dynamic_slice_in_dim(keep_mask, seq_place * shard_len, shard_len, 1)
    wide_shape = jax.ShapeDtypeStruct((D, tokens), jnp.float32)
    low_shape = jax.ShapeDtypeStruct((D, tokens), jnp.bfloat16)
    row_shape = jax.ShapeDtypeStruct((blocks, D, QB), jnp.bfloat16)
    thin_shape = jax.ShapeDtypeStruct((blocks, 1, QB), jnp.float32)
    row_result, result_grad, result_grad_low, kept_gate, line_grad = over_blocks(
        gate_kernel,
        blocks,
        [WIDE, WIDE, WIDE, ROW, THIN, THIN, COLUMN],
        [ROW, WIDE, WIDE, THIN, COLUMN],
        [row_shape, wide_shape, low_shape, thin_shape, COLUMN_SHAPE],
        "gate",
    )(
        middle,
        near_part,
        grid.shift(far_part, 1, 1),
        cotangents,
        gate_cotangent.reshape(blocks, 1, QB),
        wide(keep_local).reshape(blocks, 1, QB),
        gains[2] * gains[3],
    )
    kept_gate = kept_gate.reshape(row_count, shard_len)
    line_grad = line_grad[:, 0]
    row_result = exchange(row_result)
    far_grads = grid.shift(result_grad_low, 1, 1)

    lifted_grad = unlift(core, result_grad_low, far_grads, outer_full, slope_gate, slope_up)
    scatters = []
    for h in range(2):
        if inner_rows % 32 == 0:
            grad = weight_grad(lifted_grad, normed_two, far_states, 4, inner_rows, h)
        else:
            grad = weight_grad(lifted_grad, normed_two, far_states, 8)
            grad = grad.reshape(-1, 2, inner_rows // 2, D)[:, h]
        grad = grad.reshape([2] + batch_sizes + [inner_rows // 2, D])
        scatters.append(Scatter(grid, grad, back_orders[h]))
        lifted_grad = scatters[h].advance(lifted_grad)
    far_part = states_grad(core, inner_full, lifted_grad, 1, jnp.bfloat16)
    lifted_grad, far_part, row_result = tie(lifted_grad, far_part, row_result)
    far_part = grid.shift(far_part, 1, 1)
    near_part = states_grad(core, inner_full, lifted_grad, 0, jnp.float32)
    near_part = scatters[0].advance(near_part)
    middle_grad, middle_grad_low, feed_line = over_blocks(
        mid_kernel,
        blocks,
        [WIDE, WIDE, WIDE, WIDE, COLUMN],
        [WIDE, WIDE, COLUMN],
        [wide_shape, low_shape, COLUMN_SHAPE],
        "mid",
    )(near_part, far_part, middle, result_grad, gains[1])
    feed_line = feed_line[:, 0]

    mixed_grad = low(mm(middle_grad_low, output_full, (((0,), (1,)), ((), ()))))
    units, mixed_grad = tie(units, mixed_grad)
    row_mixed_grad = to_rows(mixed_grad)
    outer_grad = weight_grad(units, result_grad_low, far_grads, 4)
    chosen_mixed = low(mm(mixed, choose_output))
    output_grad = low(mm(chosen_mixed, middle_grad_low, (((0,), (1,)), ((), ()))))
    row_mixed_grad, output_grad, outer_grad = tie(row_mixed_grad, output_grad, outer_grad)
    outer_sum = lax.psum_scatter(outer_grad, ("y", "batch"), scatter_dimension=0, tiled=True)
    row_mixed_grad = scatters[1].advance(row_mixed_grad)
    row_grad, line_sums = attn_bwd(row_projected, row_mixed_grad, row_lse, bias_line)
    row_grad = scatters[0].advance(row_grad)
    row_grad = scatters[1].advance(row_grad)
    projected_grad = to_positions(row_grad)
    kept_states = compact(own_rank[:, :, None], row_result).T.reshape(1, 1, KEEP_CAP, D)
    one_hot_rows = jnp.stack([jnp.roll(one_hot, r, axis=0) for r in range(8)])
    table_grad = jnp.einsum(
        "hrw,rwb->hb",
        line_sums.reshape(HEADS, 8, WB),
        one_hot_rows,
        precision=lax.Precision.HIGHEST,
    )
    inner_sum0 = scatters[0].result(table_grad).reshape(inner_rows // 2, D)
    projected_grad, kept_states, table_grad, inner_sum0 = tie(
        projected_grad, kept_states, table_grad, inner_sum0
    )
    chosen_grad = low(mm(projected_grad, choose_attend))

    def swap(values, bit):
        pairs = [(index, index ^ bit) for index in range(grid.total)]
        return lax.ppermute(values, AXES, pairs)

    small_grads = [
        low(mm(chosen_grad, normed_one, (((0,), (1,)), ((), ())))),
        output_grad,
    ]
    bits = [1 << place for place in range((grid.total - 1).bit_length())]
    for index, (dim, odd_dim) in enumerate(stages[::-1]):
        count = grid.sizes[dim]
        parts = [jnp.split(grad, count, axis=0) for grad in small_grads]
        totals = [wide(part[0]) for part in parts]
        sends = [
            jnp.concatenate([part[step] for part in parts], axis=0) for step in range(1, count)
        ]
        if index > 0:
            if index == 1:
                inner_sum1 = scatters[1].result(sends[0]).reshape(inner_rows // 2, D)
                inner_sum1, *sends = tie(inner_sum1, *sends)
            if index == 2:
                outer_sum, *sends = tie(outer_sum, *sends)
            lines, *sends = tie(lines, *sends)
            lines = lines + swap(lines, bits.pop(0))
        moved = [grid.shift(send, dim, -step - 1, odd_dim) for step, send in enumerate(sends)]
        if index == 0:
            input_grad, attend_line = over_blocks(
                last_kernel,
                blocks,
                [
                    whole((3 * INNER, D)),
                    pl.BlockSpec((QB, 3 * INNER), lambda t: (t, 0)),
                    ROW,
                    WIDE,
                    COLUMN,
                ],
                [ROW, COLUMN],
                [row_shape, COLUMN_SHAPE],
                "last",
            )(attend_full, projected_grad, hidden.transpose(0, 2, 1), middle_grad, gains[0])
            attend_line = attend_line[:, 0]
            lines = jnp.stack(
                [
                    attend_line,
                    feed_line,
                    line_grad * norm_params[3],
                    line_grad * norm_params[2],
                    jnp.pad(table_grad.reshape(-1), (0, D - HEADS * BUCKETS)),
                ]
            )
        rows = totals[0].shape[0]
        for part in moved:
            totals = [totals[0] + wide(part[:rows]), totals[1] + wide(part[rows:])]
        small_grads = [low(total) for total in totals]
    while bits:
        lines = lines + swap(lines, bits.pop(0))
    input_grad = input_grad.transpose(0, 2, 1)

    inner_sum = jnp.concatenate([inner_sum0, inner_sum1], axis=0).T
    outer_sum = wide(lax.ppermute(outer_sum, AXES, swapped))
    attend_sum = totals[0].T
    output_sum = totals[1]
    norm_total = lines[:4]
    table_total = lines[4, : HEADS * BUCKETS].reshape(HEADS, BUCKETS)

    steps_done = wide(step_count[0])
    bias_one = 1.0 - MOMENT_DECAY**steps_done
    bias_two = 1.0 - SQUARE_DECAY**steps_done
    smooth_decay = (1.0 + steps_done) / (10.0 + steps_done)

    def updated(weight, first, second, grad, rate, average):
        return adam_step(
            weight, first, second, grad, rate, bias_one, bias_two, average, smooth_decay
        )

    return (
        kept_states,
        kept_gate,
        input_grad,
        *updated(
            attend_weight, attend_first, attend_second, attend_sum, RATE_ATTEND, attend_average
        ),
        *updated(
            output_weight, output_first, output_second, output_sum, RATE_OUTPUT, output_average
        ),
        *updated(inner_weight, inner_first, inner_second, inner_sum, RATE_INNER, inner_average),
        *updated(outer_weight, outer_first, outer_second, outer_sum, RATE_OUTER, outer_average),
        *updated(norm_params, norm_first, norm_second, norm_total, RATE_NORM, norm_average),
        *updated(bias_table, table_first, table_second, table_total, RATE_TABLE, table_average),
    )


def solution(mesh):
    placed = (
        P("batch", ("y", "core"), None),
        P("batch", None),
        P("batch", ("y", "core"), None, None),
        P("batch", ("y", "core")),
        P(),
        P(None, ("y", "core", "batch")),
        P(None, ("y", "core", "batch")),
        P(None, ("y", "core", "batch")),
        P(None, ("y", "core", "batch")),
        P(("y", "core", "batch"), None),
        P(("y", "core", "batch"), None),
        P(("y", "core", "batch"), None),
        P(("y", "core", "batch"), None),
        P(None, ("y", "core", "batch")),
        P(None, ("y", "core", "batch")),
        P(None, ("y", "core", "batch")),
        P(None, ("y", "core", "batch")),
        P(("y", "core", "batch"), None),
        P(("y", "core", "batch"), None),
        P(("y", "core", "batch"), None),
        P(("y", "core", "batch"), None),
        P(),
        P(),
        P(),
        P(),
        P(),
        P(),
        P(),
        P(),
    )
    devices = mesh.devices.reshape(mesh.shape["seq"] // 2, 2, mesh.shape["batch"])
    finer = jax.sharding.Mesh(devices, ("y", "core", "batch"))
    return jax.shard_map(
        functools.partial(per_device, mesh.shape["seq"], mesh.shape["batch"]),
        mesh=finer,
        in_specs=placed,
        out_specs=(
            P("batch", ("y", "core"), None, None),
            P("batch", ("y", "core")),
            P("batch", ("y", "core"), None),
            P(None, ("y", "core", "batch")),
            P(None, ("y", "core", "batch")),
            P(None, ("y", "core", "batch")),
            P(None, ("y", "core", "batch")),
            P(("y", "core", "batch"), None),
            P(("y", "core", "batch"), None),
            P(("y", "core", "batch"), None),
            P(("y", "core", "batch"), None),
            P(None, ("y", "core", "batch")),
            P(None, ("y", "core", "batch")),
            P(None, ("y", "core", "batch")),
            P(None, ("y", "core", "batch")),
            P(("y", "core", "batch"), None),
            P(("y", "core", "batch"), None),
            P(("y", "core", "batch"), None),
            P(("y", "core", "batch"), None),
            P(),
            P(),
            P(),
            P(),
            P(),
            P(),
            P(),
            P(),
        ),
        check_vma=False,
    )
```

```python
import functools

import jax
import jax.numpy as jnp
from jax import lax
from jax.experimental import pallas as pl
from jax.experimental.pallas import tpu as pltpu
from jax.sharding import PartitionSpec as P

D = 1472
HEADS = 6
HEAD_DIM = 64
FF = 3584
BUCKETS = 32
LEN = 1024
INNER = 384
KEEP_CAP = 768


EPSILON = 1e-06
GATE_RANGE = -30.0
MOMENT_DECAY = 0.9
SQUARE_DECAY = 0.999
ADAM_FLOOR = 1e-08
WEIGHT_DECAY = 0.01
RATE_ATTEND = 0.02
RATE_OUTPUT = 4.0
RATE_INNER = 0.06
RATE_OUTER = 0.04
RATE_NORM = 0.5
RATE_TABLE = 1.0
far_edges = (12, 16, 23, 32, 46, 64, 91)
AXES = ("y", "core", "batch")
FREE = pl.CostEstimate(flops=0, bytes_accessed=0, transcendentals=0)
QB = 256
WB = 2048
MIB = 2**20
NT = (((1,), (1,)), ((), ()))
TN = (((0,), (0,)), ((), ()))


def cost(micros):
    return pl.CostEstimate(flops=micros * 10**9, bytes_accessed=0, transcendentals=0)


def mm(a,b,dims=(((1,),(0,)),((),()))):
    return lax.dot_general(a,b,dims,preferred_element_type=jnp.float32)
def head_mask(shape,h):
    lane=lax.broadcasted_iota(jnp.int32,shape,1)
    return (lane<64) if h==0 else (lane>=64)
def fill_bias(t_ref,b_ref):
    for h in range(2):
        row=jnp.broadcast_to(t_ref[0,h:h+1,:],(QB,WB))
        b_ref[h]=pltpu.roll(row,0,1,stride=1,stride_axis=0)
def fwd_kernel(q_ref,k_ref,v_ref,t_ref,o_ref,l_ref,b_ref):
    fill_bias(t_ref,b_ref)
    k=k_ref[...]; v=v_ref[...]
    nq=LEN//QB
    def body(i,_):
        rows=pl.ds(pl.multiple_of(i*QB,QB),QB)
        qb=q_ref[rows,:]
        cols=pl.ds(pl.multiple_of((nq-1-i)*QB,QB),LEN)
        outs=[];ls=[]
        for h in range(2):
            qm=jnp.where(head_mask(qb.shape,h),qb,jnp.zeros_like(qb))
            s=mm(qm,k,NT)+b_ref[h,:,cols]
            m=jnp.max(s,-1,keepdims=True)
            e=jnp.exp(s-m)
            l=jnp.sum(e,-1,keepdims=True)
            o=mm((e*(1.0/l)).astype(jnp.bfloat16),v)
            outs.append(o); ls.append(m+jnp.log(l))
        msk=head_mask(outs[0].shape,0)
        o_ref[rows,:]=jnp.where(msk,outs[0],outs[1]).astype(o_ref.dtype)
        l_ref[rows,:]=jnp.where(msk,jnp.broadcast_to(ls[0],outs[0].shape),jnp.broadcast_to(ls[1],outs[0].shape))
        return 0
    lax.fori_loop(0,nq,body,0)
def attn_fwd(qkv,tvec):
    n=INNER//128
    return pl.pallas_call(fwd_kernel,grid=(n,),
        in_specs=[pl.BlockSpec((LEN,128),lambda h:(0,h)),pl.BlockSpec((LEN,128),lambda h:(0,n+h)),pl.BlockSpec((LEN,128),lambda h:(0,2*n+h)),
                  pl.BlockSpec((1,2,WB),lambda h:(h,0,0))],
        out_specs=[pl.BlockSpec((LEN,128),lambda h:(0,h)),pl.BlockSpec((LEN,128),lambda h:(0,h))],
        out_shape=[jax.ShapeDtypeStruct((LEN,INNER),jnp.bfloat16),jax.ShapeDtypeStruct((LEN,INNER),jnp.float32)],
        scratch_shapes=[pltpu.VMEM((2,QB,WB),jnp.float32)],
        compiler_params=pltpu.CompilerParams(vmem_limit_bytes=48*2**20),
        cost_estimate=cost(3),
        name="attn_fwd")(qkv,qkv,qkv,tvec)
def bwd_kernel(q_ref,k_ref,v_ref,g_ref,l_ref,t_ref,o_ref,dt_ref,b_ref,db_ref,dk_ref,dv_ref):
    fill_bias(t_ref,b_ref)
    db_ref[...]=jnp.zeros_like(db_ref)
    dk_ref[...]=jnp.zeros_like(dk_ref)
    dv_ref[...]=jnp.zeros_like(dv_ref)
    k=k_ref[...]; v=v_ref[...]
    nq=LEN//QB
    hp=pl.program_id(0)
    def body(i,_):
        rows=pl.ds(pl.multiple_of(i*QB,QB),QB)
        qb=q_ref[rows,:]; gb=g_ref[rows,:]; lb=l_ref[rows,:]
        cols=pl.ds(pl.multiple_of((nq-1-i)*QB,QB),LEN)
        dqs=[]
        for h in range(2):
            hm=head_mask(qb.shape,h)
            qm=jnp.where(hm,qb,jnp.zeros_like(qb)); gm=jnp.where(hm,gb,jnp.zeros_like(gb))
            s=mm(qm,k,NT)+b_ref[h,:,cols]
            p=jnp.exp(s-lb[:,64*h:64*h+1])
            dp=mm(gm,v,NT)
            t=p*dp
            d=jnp.sum(t,-1,keepdims=True)
            ds=(t-p*d)
            db_ref[h,:,cols]+=ds
            ds=ds.astype(jnp.bfloat16)
            dv_ref[...]+=mm(p.astype(jnp.bfloat16),gm,TN)
            dk_ref[...]+=mm(ds,qm,TN)
            dqs.append(mm(ds,k))
        o_ref[rows,pl.ds(pl.multiple_of(hp*128,128),128)]=jnp.where(head_mask(dqs[0].shape,0),dqs[0],dqs[1]).astype(o_ref.dtype)
        return 0
    lax.fori_loop(0,nq,body,0)
    o_ref[:,pl.ds(pl.multiple_of(INNER+hp*128,128),128)]=dk_ref[...].astype(o_ref.dtype)
    o_ref[:,pl.ds(pl.multiple_of(2*INNER+hp*128,128),128)]=dv_ref[...].astype(o_ref.dtype)
    for h in range(2):
        rows=QB//2
        while rows>=8:
            db_ref[h,:rows,:]=db_ref[h,:rows,:]+pltpu.roll(db_ref[h,rows:2*rows,:],WB-rows,1)
            rows//=2
        dt_ref[0,h]=db_ref[h,:8,:]
def attn_bwd(qkv,grad,lse,tvec):
    n=INNER//128
    return pl.pallas_call(bwd_kernel,grid=(n,),
        in_specs=[pl.BlockSpec((LEN,128),lambda h:(0,h)),pl.BlockSpec((LEN,128),lambda h:(0,n+h)),pl.BlockSpec((LEN,128),lambda h:(0,2*n+h)),
                  pl.BlockSpec((LEN,128),lambda h:(0,h)),pl.BlockSpec((LEN,128),lambda h:(0,h)),
                  pl.BlockSpec((1,2,WB),lambda h:(h,0,0))],
        out_specs=[pl.BlockSpec((LEN,3*INNER),lambda h:(0,0)),pl.BlockSpec((1,2,8,WB),lambda h:(h,0,0,0))],
        out_shape=[jax.ShapeDtypeStruct((LEN,3*INNER),jnp.bfloat16),jax.ShapeDtypeStruct((n,2,8,WB),jnp.float32)],
        scratch_shapes=[pltpu.VMEM((2,QB,WB),jnp.float32),pltpu.VMEM((2,QB,WB),jnp.float32),pltpu.VMEM((LEN,128),jnp.float32),pltpu.VMEM((LEN,128),jnp.float32)],
        compiler_params=pltpu.CompilerParams(vmem_limit_bytes=48*2**20),
        cost_estimate=cost(5),
        name="attn_bwd")(qkv,qkv,qkv,grad,lse,tvec)


def bucket_of_offset(offset):
    distance = jnp.abs(offset)
    far_bucket = jnp.full(distance.shape, 8, jnp.int32)
    for edge_value in far_edges:
        far_bucket = far_bucket + (distance >= edge_value).astype(jnp.int32)
    near_bucket = jnp.where(distance < 8, distance, far_bucket)
    return near_bucket + jnp.where(offset > 0, 16, 0)


def adam_step(weight, first, second, grad, rate, bias_one, bias_two, average, smooth_decay):
    first_new = MOMENT_DECAY * first + (1.0 - MOMENT_DECAY) * grad
    second_new = SQUARE_DECAY * second + (1.0 - SQUARE_DECAY) * grad * grad
    direction = first_new / bias_one / (jnp.sqrt(second_new / bias_two) + ADAM_FLOOR)
    weight_new = weight - rate * (direction + WEIGHT_DECAY * weight)
    average_new = smooth_decay * average + (1.0 - smooth_decay) * weight_new
    return (weight_new, first_new, second_new, average_new)


def low(values):
    return values.astype(jnp.bfloat16)


def wide(values):
    return values.astype(jnp.float32)


def tie(*values):
    return lax.optimization_barrier(values)


class Grid:
    def __init__(self, seq_count, batch_count):
        if batch_count == 8:
            digits = [4, 2]
        else:
            digits, rest = [], batch_count
            while rest % 4 == 0:
                digits, rest = [4] + digits, rest // 4
            if rest > 1:
                digits = [rest] + digits
        self.sizes = [seq_count // 2, 2] + digits
        self.total = seq_count * batch_count
        self.batch_dims = list(range(2, len(self.sizes)))
        self.swaps = self.sizes[-1] == self.sizes[0]

    def split(self, index):
        out = []
        for size in reversed(self.sizes):
            out.append(index % size)
            index = index // size
        return out[::-1]

    def join(self, coords):
        index = 0
        for size, coord in zip(self.sizes, coords):
            index = index * size + coord
        return index

    def shift(self, values, dim, step, odd_dim=None):
        pairs = []
        for index in range(self.total):
            coords = self.split(index)
            along = dim if odd_dim is None or coords[1] == 0 else odd_dim
            coords[along] = (coords[along] + step) % self.sizes[along]
            pairs.append((index, self.join(coords)))
        return lax.ppermute(values, AXES, pairs)

    def mine(self):
        return self.split(lax.axis_index(AXES))

    def small_stages(self):
        first = [(dim, dim) for dim in self.batch_dims[:-1]]
        x, y = self.batch_dims[-1], 0
        if self.swaps:
            return first + [(x, y), (y, x), (1, 1)]
        return first + [(x, x), (y, y), (1, 1)]

    def small_owner(self):
        stages = self.small_stages()
        rest = jnp.arange(self.total, dtype=jnp.int32)
        steps = []
        for dim, _ in stages:
            steps.append(rest % self.sizes[dim])
            rest = rest // self.sizes[dim]
        mine = self.mine()
        core = (mine[1] + steps[-1]) % 2
        coords = list(mine)
        coords[1] = core
        for (dim, odd_dim), step in zip(stages[:-1], steps[:-1]):
            if dim == odd_dim:
                coords[dim] = (coords[dim] - step) % self.sizes[dim]
            else:
                for this, other in ((dim, 0), (odd_dim, 1)):
                    coords[this] = jnp.where(
                        core == other, (coords[this] - step) % self.sizes[this], coords[this]
                    )
        return self.join(coords)


def absolute(parts, place):
    count = len(parts)
    if count == 2:
        first = place == 0
        return [jnp.where(first, parts[0], parts[1]), jnp.where(first, parts[1], parts[0])]
    return [
        lax.select_n(lax.rem(place - j + count, count), *parts) for j in range(count)
    ]


class Scatter:
    def __init__(self, grid, pieces, order):
        self.grid = grid
        self.plan = list(order)
        self.sent = False
        self.start(pieces)

    def start(self, pieces):
        dim = self.plan[0]
        count = self.grid.sizes[dim]
        axis = max(dim - 1, 0)
        place = self.grid.mine()[dim]
        if count == 2:
            parts = [lax.slice_in_dim(pieces, j, j + 1, axis=axis) for j in range(count)]
            self.parts = absolute(parts, place)
        else:
            self.parts = [
                lax.dynamic_slice_in_dim(pieces, lax.rem(place - j + count, count), 1, axis)
                for j in range(count)
            ]

    def settle(self):
        self.plan.pop(0)
        total = wide(self.parts[0])
        for part in self.parts[1:]:
            total = total + wide(part)
        self.total = low(total) if self.plan else total
        self.sent = False
        if self.plan:
            self.start(self.total)

    def send(self):
        dim = self.plan[0]
        for step in range(1, len(self.parts)):
            self.parts[step] = self.grid.shift(self.parts[step], dim, -step)
        self.sent = True

    def advance(self, *values):
        if self.sent:
            _, *self.parts = tie(values[0], *self.parts)
            self.settle()
        if self.plan:
            count = len(self.parts) - 1
            tied = tie(*values, *self.parts[1:])
            self.parts[1:] = tied[-count:]
            values = tied[:-count]
            self.send()
        return values[0] if len(values) == 1 else values

    def collect(self, value):
        _, *self.parts = tie(value, *self.parts)
        self.settle()
        value, *self.parts = tie(value, *self.parts)
        return value

    def result(self, value):
        if self.sent:
            _, *self.parts = tie(value, *self.parts)
        while self.plan:
            if self.sent:
                self.settle()
            if self.plan:
                self.send()
        return self.total


def exchange(values):
    return lax.all_to_all(values, ("y", "core"), split_axis=0, concat_axis=0, tiled=True)


def pick(near_ref, far_ref):
    step = pl.program_id(0)
    return jnp.where(step < pl.num_programs(0) // 2, near_ref[...], far_ref[...])


def pair_specs(rows, blocks):
    return [
        pl.BlockSpec((rows, QB), lambda t, core: (0, jnp.minimum(t, blocks - 1))),
        pl.BlockSpec((rows, QB), lambda t, core: (0, jnp.maximum(t - blocks, 0))),
    ]


def by_core(kernel, grid, in_specs, out_specs, out_shape, name, micros):
    return pl.pallas_call(
        lambda core_ref, *refs: kernel(*refs),
        grid_spec=pltpu.PrefetchScalarGridSpec(
            num_scalar_prefetch=1, grid=grid, in_specs=in_specs, out_specs=out_specs
        ),
        out_shape=out_shape,
        compiler_params=pltpu.CompilerParams(vmem_limit_bytes=56 * MIB),
        cost_estimate=cost(micros),
        name=name,
    )


def weight_spec(first):
    return pl.BlockSpec((1, FF // 2, D), lambda t, core: (first + core[0], 0, 0))


def token_spec(rows, first=0):
    return pl.BlockSpec((rows, QB), lambda t, core: (0, first + t))


def lift_kernel(near_ref, far_ref, g_ref, u_ref, units_ref, da_ref, db_ref):
    block = pick(near_ref, far_ref)
    rows = units_ref.shape[0] // 2
    for part in range(2):
        here = slice(part * rows, (part + 1) * rows)
        gate = mm(g_ref[0, here, :], block)
        up = mm(u_ref[0, here, :], block)
        root = 0.7978845608028654
        square = gate * gate
        inside = jnp.tanh(root * gate * (1.0 + 0.044715 * square))
        half = 0.5 * (1.0 + inside)
        active = gate * half
        slope = half + 0.5 * gate * (1.0 - inside * inside) * (
            root * (1.0 + 3.0 * 0.044715 * square)
        )
        units_ref[here, :] = low(active * up)
        da_ref[here, :] = low(up * slope)
        db_ref[here, :] = low(active)


def lift(core, near, far, inner_full):
    tokens = 2 * near.shape[1]
    blocks = near.shape[1] // QB
    out = jax.ShapeDtypeStruct((FF // 2, tokens), jnp.bfloat16)
    return by_core(
        lift_kernel,
        (2 * blocks,),
        pair_specs(D, blocks) + [weight_spec(0), weight_spec(2)],
        [token_spec(FF // 2)] * 3,
        [out] * 3,
        "lift",
        5,
    )(core, near, far, inner_full, inner_full)


def unlift_kernel(near_ref, far_ref, w_ref, da_ref, db_ref, out_ref):
    half = w_ref.shape[1]
    units_grad = mm(w_ref[0], pick(near_ref, far_ref))
    out_ref[:half, :] = low(units_grad * wide(da_ref[...]))
    out_ref[half:, :] = low(units_grad * wide(db_ref[...]))


def unlift(core, near, far, outer_full, slope_gate, slope_up):
    tokens = 2 * near.shape[1]
    blocks = near.shape[1] // QB
    return by_core(
        unlift_kernel,
        (2 * blocks,),
        pair_specs(D, blocks) + [weight_spec(0)] + [token_spec(FF // 2)] * 2,
        token_spec(FF),
        jax.ShapeDtypeStruct((FF, tokens), jnp.bfloat16),
        "unlift",
        3,
    )(core, near, far, outer_full, slope_gate, slope_up)


def lower_kernel(w_ref, units_ref, out_ref):
    out_ref[...] = mm(w_ref[0], units_ref[...], TN).astype(out_ref.dtype)


def lower(core, outer_full, units, first, dtype):
    tokens = units.shape[1] // 2
    return by_core(
        lower_kernel,
        (tokens // QB,),
        [weight_spec(0), token_spec(FF // 2, first * (tokens // QB))],
        token_spec(D),
        jax.ShapeDtypeStruct((D, tokens), dtype),
        "lower",
        2,
    )(core, outer_full, units)


def states_grad_kernel(g_ref, u_ref, grad_ref, out_ref):
    half = g_ref.shape[1]
    total = mm(g_ref[0], grad_ref[:half, :], TN)
    out_ref[...] = (total + mm(u_ref[0], grad_ref[half:, :], TN)).astype(out_ref.dtype)


def states_grad(core, inner_full, lifted_grad, first, dtype):
    tokens = lifted_grad.shape[1] // 2
    return by_core(
        states_grad_kernel,
        (tokens // QB,),
        [weight_spec(0), weight_spec(2), token_spec(FF, first * (tokens // QB))],
        token_spec(D),
        jax.ShapeDtypeStruct((D, tokens), dtype),
        "states_grad",
        0,
    )(core, inner_full, inner_full, lifted_grad)


def whole(shape):
    return pl.BlockSpec(shape, lambda *_: (0,) * len(shape))


def weight_grad_kernel(block, half, left_ref, near_ref, far_ref, out_ref):
    tokens = near_ref.shape[1]
    left = left_ref[...]
    if half is not None:
        starts = range(half * (block // 2), left.shape[0], block)
        left = jnp.concatenate([left[start : start + block // 2] for start in starts], axis=0)
    total = mm(left[:, :tokens], near_ref[...], NT)
    out_ref[...] = low(total + mm(left[:, tokens:], far_ref[...], NT))


def weight_grad(left, near, far, count, block=None, half=None):
    tokens = near.shape[1]
    tile = left.shape[0] // count
    rows = tile if half is None else tile // 2
    return pl.pallas_call(
        functools.partial(weight_grad_kernel, block, half),
        grid=(count,),
        in_specs=[
            pl.BlockSpec((tile, 2 * tokens), lambda f: (f, 0)),
            whole((D, tokens)),
            whole((D, tokens)),
        ],
        out_specs=pl.BlockSpec((rows, D), lambda f: (f, 0)),
        out_shape=jax.ShapeDtypeStruct((count * rows, D), jnp.bfloat16),
        compiler_params=pltpu.CompilerParams(vmem_limit_bytes=56 * MIB),
        cost_estimate=cost(2),
        name="weight_grad",
    )(left, near, far)


def scale_of(values):
    return lax.rsqrt(jnp.mean(values * values, axis=0, keepdims=True) + EPSILON)


def add_line(line_ref, values):
    total = jnp.sum(values, axis=1, keepdims=True)

    @pl.when(pl.program_id(0) == 0)
    def _():
        line_ref[...] = total

    @pl.when(pl.program_id(0) > 0)
    def _():
        line_ref[...] += total


def back_through_norm(values, scale, weighted):
    inner_mean = jnp.mean(weighted * values, axis=0, keepdims=True)
    return scale * weighted - values * (scale * scale * scale * inner_mean)


def gate_kernel(
    middle_ref, near_ref, far_ref, state_ref, cot_ref, keep_ref, gain_ref,
    result_ref, grad_ref, low_ref, gate_ref, line_ref,
):
    result = middle_ref[...] + near_ref[...] + wide(far_ref[...])
    result_ref[0] = low(result)
    scale = scale_of(result)
    gain = gain_ref[...]
    dot = jnp.sum(result * gain, axis=0, keepdims=True)
    squashed = jax.nn.sigmoid(dot * scale)
    keep = keep_ref[0]
    gate_ref[0] = GATE_RANGE * squashed * keep
    logit_grad = cot_ref[0] * keep * GATE_RANGE * squashed * (1.0 - squashed)
    share = logit_grad * scale
    grad = (
        wide(state_ref[0]) + share * gain - result * (share * scale * scale * dot * (1.0 / D))
    )
    grad_ref[...] = grad
    low_ref[...] = low(grad)
    add_line(line_ref, share * result)


def mid_kernel(near_ref, far_ref, middle_ref, grad_ref, gain_ref, out_ref, low_ref, line_ref):
    normed_grad = near_ref[...] + wide(far_ref[...])
    middle = middle_ref[...]
    scale = scale_of(middle)
    total = grad_ref[...] + back_through_norm(middle, scale, normed_grad * gain_ref[...])
    out_ref[...] = total
    low_ref[...] = low(total)
    add_line(line_ref, normed_grad * middle * scale)


def last_kernel(w_ref, projected_ref, hidden_ref, grad_ref, gain_ref, out_ref, line_ref):
    normed_grad = mm(w_ref[...], projected_ref[...], (((0,), (1,)), ((), ())))
    hidden = wide(hidden_ref[0])
    scale = scale_of(hidden)
    out_ref[0] = low(
        grad_ref[...] + back_through_norm(hidden, scale, normed_grad * gain_ref[...])
    )
    add_line(line_ref, normed_grad * hidden * scale)


WIDE = pl.BlockSpec((D, QB), lambda t: (0, t))
ROW = pl.BlockSpec((1, D, QB), lambda t: (t, 0, 0))
THIN = pl.BlockSpec((1, 1, QB), lambda t: (t, 0, 0))
COLUMN = pl.BlockSpec((D, 1), lambda t: (0, 0))
COLUMN_SHAPE = jax.ShapeDtypeStruct((D, 1), jnp.float32)


def over_blocks(kernel, count, in_specs, out_specs, out_shape, name):
    return pl.pallas_call(
        kernel,
        grid=(count,),
        in_specs=in_specs,
        out_specs=out_specs,
        out_shape=out_shape,
        compiler_params=pltpu.CompilerParams(vmem_limit_bytes=56 * MIB),
        cost_estimate=cost(0),
        name=name,
    )


def spread_kernel(rank_ref, cot_ref, out_ref):
    slot = lax.broadcasted_iota(jnp.int32, (KEEP_CAP, QB), 0)
    chosen = low(jnp.where(slot == rank_ref[0], 1.0, 0.0))
    out_ref[0] = low(mm(cot_ref[...], chosen))


def spread(rank, cotangent):
    blocks = rank.shape[0]
    return pl.pallas_call(
        spread_kernel,
        grid=(blocks,),
        in_specs=[
            pl.BlockSpec((1, 1, QB), lambda i: (i, 0, 0)),
            pl.BlockSpec((D, KEEP_CAP), lambda i: (0, 0)),
        ],
        out_specs=pl.BlockSpec((1, D, QB), lambda i: (i, 0, 0)),
        out_shape=jax.ShapeDtypeStruct((blocks, D, QB), jnp.bfloat16),
        compiler_params=pltpu.CompilerParams(vmem_limit_bytes=40 * MIB),
        cost_estimate=cost(1),
        name="spread",
    )(rank, cotangent)


def compact_kernel(rank_ref, rows_ref, out_ref, sum_ref):
    slot = lax.broadcasted_iota(jnp.int32, (QB, KEEP_CAP), 1)
    chosen = low(jnp.where(slot == rank_ref[0], 1.0, 0.0))
    part = mm(rows_ref[0], chosen)

    @pl.when(pl.program_id(0) == 0)
    def _():
        sum_ref[...] = part

    @pl.when(pl.program_id(0) > 0)
    def _():
        sum_ref[...] += part

    @pl.when(pl.program_id(0) == pl.num_programs(0) - 1)
    def _():
        out_ref[...] = low(sum_ref[...])


def compact(rank, rows):
    blocks = rank.shape[0]
    return pl.pallas_call(
        compact_kernel,
        grid=(blocks,),
        in_specs=[
            pl.BlockSpec((1, QB, 1), lambda i: (i, 0, 0)),
            pl.BlockSpec((1, D, QB), lambda i: (i, 0, 0)),
        ],
        out_specs=pl.BlockSpec((D, KEEP_CAP), lambda i: (0, 0)),
        out_shape=jax.ShapeDtypeStruct((D, KEEP_CAP), jnp.bfloat16),
        scratch_shapes=[pltpu.VMEM((D, KEEP_CAP), jnp.float32)],
        compiler_params=pltpu.CompilerParams(vmem_limit_bytes=40 * MIB),
        cost_estimate=cost(1),
        name="compact",
    )(rank, rows)


def per_device(
    seq_count,
    batch_count,
    hidden,
    keep_mask,
    states_cotangent,
    gate_cotangent,
    step_count,
    attend_weight,
    attend_first,
    attend_second,
    attend_average,
    output_weight,
    output_first,
    output_second,
    output_average,
    inner_weight,
    inner_first,
    inner_second,
    inner_average,
    outer_weight,
    outer_first,
    outer_second,
    outer_average,
    norm_params,
    norm_first,
    norm_second,
    norm_average,
    bias_table,
    table_first,
    table_second,
    table_average,
):
    grid = Grid(seq_count, batch_count)
    batch_dims = grid.batch_dims
    batch_sizes = [grid.sizes[dim] for dim in batch_dims]
    ones = (1,) * len(batch_dims)
    seq_place = lax.axis_index(("y", "core"))
    row_count, shard_len = hidden.shape[0], hidden.shape[1]
    tokens = row_count * shard_len
    attend_rows, output_rows = attend_weight.shape[1], output_weight.shape[0]
    inner_rows, outer_rows = inner_weight.shape[1], outer_weight.shape[0]
    half_ff = FF // 2

    core = lax.axis_index("core").reshape(1).astype(jnp.int32)
    small_rows = attend_rows + output_rows
    small = jnp.concatenate([low(attend_weight).T, low(output_weight)], axis=0)[None]
    stages = grid.small_stages()

    def small_stage(blocks, stage):
        dim, odd_dim = stage
        parts = [blocks] + [
            grid.shift(blocks, dim, step, odd_dim) for step in range(1, grid.sizes[dim])
        ]
        return jnp.concatenate(parts, axis=0)

    swapped = []
    for index in range(grid.total):
        y, core_place, *rest = grid.split(index)
        swapped.append((index, grid.join([core_place, y] + rest)))
    small = small_stage(small, stages[0])
    inner_piece = low(inner_weight).T
    hidden, inner_piece = tie(hidden, inner_piece)
    owner = grid.small_owner()[:, None]

    def choose_rows(rows, width):
        ids = (owner * rows + jnp.arange(rows, dtype=jnp.int32)[None, :]).reshape(1, -1)
        return low(jnp.arange(width, dtype=jnp.int32)[:, None] == ids)

    ids = jnp.arange(small_rows, dtype=jnp.int32)[None, :]
    place = jnp.where(
        ids < attend_rows,
        owner * attend_rows + ids,
        3 * INNER + owner * output_rows + ids - attend_rows,
    ).reshape(1, -1)
    choose = low(jnp.arange(4 * INNER, dtype=jnp.int32)[:, None] == place)
    choose_attend = choose_rows(attend_rows, 3 * INNER)
    choose_output = choose_rows(output_rows, INNER)
    choose_attend, choose_output = tie(choose_attend, choose_output)

    back_orders = [batch_dims[:0:-1] + [0] + batch_dims[:1], [0] + batch_dims[::-1]]

    def by_token(values):
        return values.transpose(1, 0, 2).reshape(D, tokens)

    def to_rows(values):
        width = values.shape[-1]
        return exchange(values.reshape(row_count, shard_len, width)).reshape(LEN, width)

    def to_positions(values):
        width = values.shape[-1]
        return exchange(values.reshape(seq_count, shard_len, width)).reshape(tokens, width)

    own_keep = lax.dynamic_slice_in_dim(keep_mask, seq_place, 1, 0)
    own_rank = jnp.where(own_keep > 0, jnp.cumsum(own_keep, axis=1) - 1, -1)
    own_rank = own_rank.reshape(LEN // QB, QB)

    hidden_in = wide(by_token(hidden.transpose(0, 2, 1)))

    gains = norm_params[:, :, None]
    scale_one = scale_of(hidden_in)
    normed_one = low(hidden_in * scale_one * gains[0])
    cotangents = spread(own_rank[:, None, :], states_cotangent.reshape(KEEP_CAP, D).T)
    small, normed_one = tie(small, normed_one)
    for stage in stages[1:-1]:
        small = small_stage(small, stage)
    small, inner_piece = tie(small, inner_piece)
    inner_full = lax.all_gather(inner_piece, AXES, axis=0, tiled=True)
    inner_full = inner_full.reshape(4, FF // 2, D)
    _, outer_piece = tie(small, low(outer_weight))
    outer_full = lax.all_gather(outer_piece, AXES, axis=0, tiled=True)
    outer_full = outer_full.reshape(2, FF // 2, D)
    small = small_stage(small, stages[-1]).reshape(grid.total * small_rows, D)
    attend_full = low(mm(choose[: 3 * INNER], small))
    projected = low(mm(normed_one, attend_full, (((0,), (1,)), ((), ()))))
    _, small = tie(projected, small)
    output_full = low(mm(choose[3 * INNER :], small))
    row_projected = to_rows(projected)
    window = jnp.arange(WB, dtype=jnp.int32)
    offsets = jnp.where(window >= WB - QB, window - WB, window) - (LEN - QB)
    one_hot = wide(
        bucket_of_offset(offsets)[:, None] == jnp.arange(BUCKETS, dtype=jnp.int32)[None, :]
    )
    bias_line = jnp.sum(bias_table[:, None, :] * one_hot[None], axis=-1)
    bias_line = bias_line.reshape(HEADS // 2, 2, WB)
    row_projected, output_full = tie(row_projected, output_full)
    row_mixed, row_lse = attn_fwd(row_projected, bias_line)
    mixed = to_positions(row_mixed)
    mixed, cotangents = tie(mixed, cotangents)
    cotangents, row_mixed = tie(cotangents, row_mixed)
    mixed, cotangents = tie(mixed, cotangents)
    middle = hidden_in + mm(output_full, mixed, (((0,), (1,)), ((), ())))
    scale_two = scale_of(middle)
    normed_two = low(middle * scale_two * gains[1])
    far_states = grid.shift(normed_two, 1, 1)

    _, inner_full = tie(normed_two, inner_full)
    inner_full, cotangents = tie(inner_full, cotangents)
    cotangents = exchange(cotangents)
    units, slope_gate, slope_up = lift(core, normed_two, far_states, inner_full)
    _, outer_full = tie(units, outer_full)
    far_part = lower(core, outer_full, units, 1, jnp.bfloat16)
    units, far_part, cotangents = tie(units, far_part, cotangents)
    near_part = lower(core, outer_full, units, 0, jnp.float32)

    blocks = tokens // QB
    keep_local = lax.dynamic_slice_in_dim(keep_mask, seq_place * shard_len, shard_len, 1)
    wide_shape = jax.ShapeDtypeStruct((D, tokens), jnp.float32)
    low_shape = jax.ShapeDtypeStruct((D, tokens), jnp.bfloat16)
    row_shape = jax.ShapeDtypeStruct((blocks, D, QB), jnp.bfloat16)
    thin_shape = jax.ShapeDtypeStruct((blocks, 1, QB), jnp.float32)
    row_result, result_grad, result_grad_low, kept_gate, line_grad = over_blocks(
        gate_kernel,
        blocks,
        [WIDE, WIDE, WIDE, ROW, THIN, THIN, COLUMN],
        [ROW, WIDE, WIDE, THIN, COLUMN],
        [row_shape, wide_shape, low_shape, thin_shape, COLUMN_SHAPE],
        "gate",
    )(
        middle,
        near_part,
        grid.shift(far_part, 1, 1),
        cotangents,
        gate_cotangent.reshape(blocks, 1, QB),
        wide(keep_local).reshape(blocks, 1, QB),
        gains[2] * gains[3],
    )
    kept_gate = kept_gate.reshape(row_count, shard_len)
    line_grad = line_grad[:, 0]
    row_result = exchange(row_result)
    far_grads = grid.shift(result_grad_low, 1, 1)

    lifted_grad = unlift(core, result_grad_low, far_grads, outer_full, slope_gate, slope_up)
    scatters = []
    for h in range(2):
        if inner_rows % 32 == 0:
            grad = weight_grad(lifted_grad, normed_two, far_states, 4, inner_rows, h)
        else:
            grad = weight_grad(lifted_grad, normed_two, far_states, 8)
            grad = grad.reshape(-1, 2, inner_rows // 2, D)[:, h]
        grad = grad.reshape([2] + batch_sizes + [inner_rows // 2, D])
        scatters.append(Scatter(grid, grad, back_orders[h]))
        lifted_grad = scatters[h].advance(lifted_grad)
    far_part = states_grad(core, inner_full, lifted_grad, 1, jnp.bfloat16)
    lifted_grad, far_part, row_result = tie(lifted_grad, far_part, row_result)
    far_part = grid.shift(far_part, 1, 1)
    near_part = states_grad(core, inner_full, lifted_grad, 0, jnp.float32)
    near_part = scatters[0].collect(near_part)
    middle_grad, middle_grad_low, feed_line = over_blocks(
        mid_kernel,
        blocks,
        [WIDE, WIDE, WIDE, WIDE, COLUMN],
        [WIDE, WIDE, COLUMN],
        [wide_shape, low_shape, COLUMN_SHAPE],
        "mid",
    )(near_part, far_part, middle, result_grad, gains[1])
    feed_line = feed_line[:, 0]

    mixed_grad = low(mm(middle_grad_low, output_full, (((0,), (1,)), ((), ()))))
    units, mixed_grad = tie(units, mixed_grad)
    row_mixed_grad = to_rows(mixed_grad)
    outer_grad = weight_grad(units, result_grad_low, far_grads, 4)
    chosen_mixed = low(mm(mixed, choose_output))
    output_grad = low(mm(chosen_mixed, middle_grad_low, (((0,), (1,)), ((), ()))))
    row_mixed_grad, output_grad, outer_grad = tie(row_mixed_grad, output_grad, outer_grad)
    outer_sum = lax.psum_scatter(outer_grad, ("y", "batch"), scatter_dimension=0, tiled=True)
    row_mixed_grad = scatters[0].advance(row_mixed_grad)
    row_mixed_grad = scatters[1].advance(row_mixed_grad)
    row_grad, line_sums = attn_bwd(row_projected, row_mixed_grad, row_lse, bias_line)
    row_grad = scatters[0].advance(row_grad)
    row_grad = scatters[1].advance(row_grad)
    projected_grad = to_positions(row_grad)
    kept_states = compact(own_rank[:, :, None], row_result).T.reshape(1, 1, KEEP_CAP, D)
    one_hot_rows = jnp.stack([jnp.roll(one_hot, r, axis=0) for r in range(8)])
    table_grad = jnp.einsum(
        "hrw,rwb->hb",
        line_sums.reshape(HEADS, 8, WB),
        one_hot_rows,
        precision=lax.Precision.HIGHEST,
    )
    inner_sum0 = scatters[0].result(table_grad).reshape(inner_rows // 2, D)
    projected_grad, kept_states, table_grad, inner_sum0 = tie(
        projected_grad, kept_states, table_grad, inner_sum0
    )
    chosen_grad = low(mm(projected_grad, choose_attend))

    def swap(values, bit):
        pairs = [(index, index ^ bit) for index in range(grid.total)]
        return lax.ppermute(values, AXES, pairs)

    small_grads = [
        low(mm(chosen_grad, normed_one, (((0,), (1,)), ((), ())))),
        output_grad,
    ]
    bits = [1 << place for place in range((grid.total - 1).bit_length())]
    for index, (dim, odd_dim) in enumerate(stages[::-1]):
        count = grid.sizes[dim]
        parts = [jnp.split(grad, count, axis=0) for grad in small_grads]
        totals = [wide(part[0]) for part in parts]
        sends = [
            jnp.concatenate([part[step] for part in parts], axis=0) for step in range(1, count)
        ]
        if index > 0:
            if index == 1:
                inner_sum1 = scatters[1].result(sends[0]).reshape(inner_rows // 2, D)
                inner_sum1, *sends = tie(inner_sum1, *sends)
            if index == 2:
                outer_sum, *sends = tie(outer_sum, *sends)
            lines, *sends = tie(lines, *sends)
            lines = lines + swap(lines, bits.pop(0))
        moved = [grid.shift(send, dim, -step - 1, odd_dim) for step, send in enumerate(sends)]
        if index == 0:
            input_grad, attend_line = over_blocks(
                last_kernel,
                blocks,
                [
                    whole((3 * INNER, D)),
                    pl.BlockSpec((QB, 3 * INNER), lambda t: (t, 0)),
                    ROW,
                    WIDE,
                    COLUMN,
                ],
                [ROW, COLUMN],
                [row_shape, COLUMN_SHAPE],
                "last",
            )(attend_full, projected_grad, hidden.transpose(0, 2, 1), middle_grad, gains[0])
            attend_line = attend_line[:, 0]
            lines = jnp.stack(
                [
                    attend_line,
                    feed_line,
                    line_grad * norm_params[3],
                    line_grad * norm_params[2],
                    jnp.pad(table_grad.reshape(-1), (0, D - HEADS * BUCKETS)),
                ]
            )
        rows = totals[0].shape[0]
        for part in moved:
            totals = [totals[0] + wide(part[:rows]), totals[1] + wide(part[rows:])]
        small_grads = [low(total) for total in totals]
    while bits:
        lines = lines + swap(lines, bits.pop(0))
    input_grad = input_grad.transpose(0, 2, 1)

    inner_sum = jnp.concatenate([inner_sum0, inner_sum1], axis=0).T
    outer_sum = wide(lax.ppermute(outer_sum, AXES, swapped))
    attend_sum = totals[0].T
    output_sum = totals[1]
    norm_total = lines[:4]
    table_total = lines[4, : HEADS * BUCKETS].reshape(HEADS, BUCKETS)

    steps_done = wide(step_count[0])
    bias_one = 1.0 - MOMENT_DECAY**steps_done
    bias_two = 1.0 - SQUARE_DECAY**steps_done
    smooth_decay = (1.0 + steps_done) / (10.0 + steps_done)

    def updated(weight, first, second, grad, rate, average):
        return adam_step(
            weight, first, second, grad, rate, bias_one, bias_two, average, smooth_decay
        )

    return (
        kept_states,
        kept_gate,
        input_grad,
        *updated(
            attend_weight, attend_first, attend_second, attend_sum, RATE_ATTEND, attend_average
        ),
        *updated(
            output_weight, output_first, output_second, output_sum, RATE_OUTPUT, output_average
        ),
        *updated(inner_weight, inner_first, inner_second, inner_sum, RATE_INNER, inner_average),
        *updated(outer_weight, outer_first, outer_second, outer_sum, RATE_OUTER, outer_average),
        *updated(norm_params, norm_first, norm_second, norm_total, RATE_NORM, norm_average),
        *updated(bias_table, table_first, table_second, table_total, RATE_TABLE, table_average),
    )


def solution(mesh):
    placed = (
        P("batch", ("y", "core"), None),
        P("batch", None),
        P("batch", ("y", "core"), None, None),
        P("batch", ("y", "core")),
        P(),
        P(None, ("y", "core", "batch")),
        P(None, ("y", "core", "batch")),
        P(None, ("y", "core", "batch")),
        P(None, ("y", "core", "batch")),
        P(("y", "core", "batch"), None),
        P(("y", "core", "batch"), None),
        P(("y", "core", "batch"), None),
        P(("y", "core", "batch"), None),
        P(None, ("y", "core", "batch")),
        P(None, ("y", "core", "batch")),
        P(None, ("y", "core", "batch")),
        P(None, ("y", "core", "batch")),
        P(("y", "core", "batch"), None),
        P(("y", "core", "batch"), None),
        P(("y", "core", "batch"), None),
        P(("y", "core", "batch"), None),
        P(),
        P(),
        P(),
        P(),
        P(),
        P(),
        P(),
        P(),
    )
    devices = mesh.devices.reshape(mesh.shape["seq"] // 2, 2, mesh.shape["batch"])
    finer = jax.sharding.Mesh(devices, ("y", "core", "batch"))
    return jax.shard_map(
        functools.partial(per_device, mesh.shape["seq"], mesh.shape["batch"]),
        mesh=finer,
        in_specs=placed,
        out_specs=(
            P("batch", ("y", "core"), None, None),
            P("batch", ("y", "core")),
            P("batch", ("y", "core"), None),
            P(None, ("y", "core", "batch")),
            P(None, ("y", "core", "batch")),
            P(None, ("y", "core", "batch")),
            P(None, ("y", "core", "batch")),
            P(("y", "core", "batch"), None),
            P(("y", "core", "batch"), None),
            P(("y", "core", "batch"), None),
            P(("y", "core", "batch"), None),
            P(None, ("y", "core", "batch")),
            P(None, ("y", "core", "batch")),
            P(None, ("y", "core", "batch")),
            P(None, ("y", "core", "batch")),
            P(("y", "core", "batch"), None),
            P(("y", "core", "batch"), None),
            P(("y", "core", "batch"), None),
            P(("y", "core", "batch"), None),
            P(),
            P(),
            P(),
            P(),
            P(),
            P(),
            P(),
            P(),
        ),
        check_vma=False,
    )
```

```python
import functools

import jax
import jax.numpy as jnp
from jax import lax
from jax.experimental import pallas as pl
from jax.experimental.pallas import tpu as pltpu
from jax.sharding import PartitionSpec as P

D = 1472
HEADS = 6
HEAD_DIM = 64
FF = 3584
BUCKETS = 32
LEN = 1024
INNER = 384
KEEP_CAP = 768


EPSILON = 1e-06
GATE_RANGE = -30.0
MOMENT_DECAY = 0.9
SQUARE_DECAY = 0.999
ADAM_FLOOR = 1e-08
WEIGHT_DECAY = 0.01
RATE_ATTEND = 0.02
RATE_OUTPUT = 4.0
RATE_INNER = 0.06
RATE_OUTER = 0.04
RATE_NORM = 0.5
RATE_TABLE = 1.0
far_edges = (12, 16, 23, 32, 46, 64, 91)
AXES = ("y", "core", "batch")
FREE = pl.CostEstimate(flops=0, bytes_accessed=0, transcendentals=0)
QB = 256
WB = 2048
MIB = 2**20
NT = (((1,), (1,)), ((), ()))
TN = (((0,), (0,)), ((), ()))


def cost(micros):
    return pl.CostEstimate(flops=micros * 10**9, bytes_accessed=0, transcendentals=0)


def mm(a,b,dims=(((1,),(0,)),((),()))):
    return lax.dot_general(a,b,dims,preferred_element_type=jnp.float32)
def head_mask(shape,h):
    lane=lax.broadcasted_iota(jnp.int32,shape,1)
    return (lane<64) if h==0 else (lane>=64)
def fill_bias(t_ref,b_ref):
    for h in range(2):
        row=jnp.broadcast_to(t_ref[0,h:h+1,:],(QB,WB))
        b_ref[h]=pltpu.roll(row,0,1,stride=1,stride_axis=0)
def fwd_kernel(q_ref,k_ref,v_ref,t_ref,o_ref,l_ref,b_ref):
    fill_bias(t_ref,b_ref)
    k=k_ref[...]; v=v_ref[...]
    nq=LEN//QB
    def body(i,_):
        rows=pl.ds(pl.multiple_of(i*QB,QB),QB)
        qb=q_ref[rows,:]
        cols=pl.ds(pl.multiple_of((nq-1-i)*QB,QB),LEN)
        outs=[];ls=[]
        for h in range(2):
            qm=jnp.where(head_mask(qb.shape,h),qb,jnp.zeros_like(qb))
            s=mm(qm,k,NT)+b_ref[h,:,cols]
            m=jnp.max(s,-1,keepdims=True)
            e=jnp.exp(s-m)
            l=jnp.sum(e,-1,keepdims=True)
            o=mm((e*(1.0/l)).astype(jnp.bfloat16),v)
            outs.append(o); ls.append(m+jnp.log(l))
        msk=head_mask(outs[0].shape,0)
        o_ref[rows,:]=jnp.where(msk,outs[0],outs[1]).astype(o_ref.dtype)
        l_ref[rows,:]=jnp.where(msk,jnp.broadcast_to(ls[0],outs[0].shape),jnp.broadcast_to(ls[1],outs[0].shape))
        return 0
    lax.fori_loop(0,nq,body,0)
def attn_fwd(qkv,tvec):
    n=INNER//128
    return pl.pallas_call(fwd_kernel,grid=(n,),
        in_specs=[pl.BlockSpec((LEN,128),lambda h:(0,h)),pl.BlockSpec((LEN,128),lambda h:(0,n+h)),pl.BlockSpec((LEN,128),lambda h:(0,2*n+h)),
                  pl.BlockSpec((1,2,WB),lambda h:(h,0,0))],
        out_specs=[pl.BlockSpec((LEN,128),lambda h:(0,h)),pl.BlockSpec((LEN,128),lambda h:(0,h))],
        out_shape=[jax.ShapeDtypeStruct((LEN,INNER),jnp.bfloat16),jax.ShapeDtypeStruct((LEN,INNER),jnp.float32)],
        scratch_shapes=[pltpu.VMEM((2,QB,WB),jnp.float32)],
        compiler_params=pltpu.CompilerParams(vmem_limit_bytes=48*2**20),
        cost_estimate=cost(3),
        name="attn_fwd")(qkv,qkv,qkv,tvec)
def bwd_kernel(q_ref,k_ref,v_ref,g_ref,l_ref,t_ref,o_ref,dt_ref,b_ref,db_ref,dk_ref,dv_ref):
    fill_bias(t_ref,b_ref)
    db_ref[...]=jnp.zeros_like(db_ref)
    dk_ref[...]=jnp.zeros_like(dk_ref)
    dv_ref[...]=jnp.zeros_like(dv_ref)
    k=k_ref[...]; v=v_ref[...]
    nq=LEN//QB
    hp=pl.program_id(0)
    def body(i,_):
        rows=pl.ds(pl.multiple_of(i*QB,QB),QB)
        qb=q_ref[rows,:]; gb=g_ref[rows,:]; lb=l_ref[rows,:]
        cols=pl.ds(pl.multiple_of((nq-1-i)*QB,QB),LEN)
        dqs=[]
        for h in range(2):
            hm=head_mask(qb.shape,h)
            qm=jnp.where(hm,qb,jnp.zeros_like(qb)); gm=jnp.where(hm,gb,jnp.zeros_like(gb))
            s=mm(qm,k,NT)+b_ref[h,:,cols]
            p=jnp.exp(s-lb[:,64*h:64*h+1])
            dp=mm(gm,v,NT)
            t=p*dp
            d=jnp.sum(t,-1,keepdims=True)
            ds=(t-p*d)
            db_ref[h,:,cols]+=ds
            ds=ds.astype(jnp.bfloat16)
            dv_ref[...]+=mm(p.astype(jnp.bfloat16),gm,TN)
            dk_ref[...]+=mm(ds,qm,TN)
            dqs.append(mm(ds,k))
        o_ref[rows,pl.ds(pl.multiple_of(hp*128,128),128)]=jnp.where(head_mask(dqs[0].shape,0),dqs[0],dqs[1]).astype(o_ref.dtype)
        return 0
    lax.fori_loop(0,nq,body,0)
    o_ref[:,pl.ds(pl.multiple_of(INNER+hp*128,128),128)]=dk_ref[...].astype(o_ref.dtype)
    o_ref[:,pl.ds(pl.multiple_of(2*INNER+hp*128,128),128)]=dv_ref[...].astype(o_ref.dtype)
    for h in range(2):
        rows=QB//2
        while rows>=8:
            db_ref[h,:rows,:]=db_ref[h,:rows,:]+pltpu.roll(db_ref[h,rows:2*rows,:],WB-rows,1)
            rows//=2
        dt_ref[0,h]=db_ref[h,:8,:]
def attn_bwd(qkv,grad,lse,tvec):
    n=INNER//128
    return pl.pallas_call(bwd_kernel,grid=(n,),
        in_specs=[pl.BlockSpec((LEN,128),lambda h:(0,h)),pl.BlockSpec((LEN,128),lambda h:(0,n+h)),pl.BlockSpec((LEN,128),lambda h:(0,2*n+h)),
                  pl.BlockSpec((LEN,128),lambda h:(0,h)),pl.BlockSpec((LEN,128),lambda h:(0,h)),
                  pl.BlockSpec((1,2,WB),lambda h:(h,0,0))],
        out_specs=[pl.BlockSpec((LEN,3*INNER),lambda h:(0,0)),pl.BlockSpec((1,2,8,WB),lambda h:(h,0,0,0))],
        out_shape=[jax.ShapeDtypeStruct((LEN,3*INNER),jnp.bfloat16),jax.ShapeDtypeStruct((n,2,8,WB),jnp.float32)],
        scratch_shapes=[pltpu.VMEM((2,QB,WB),jnp.float32),pltpu.VMEM((2,QB,WB),jnp.float32),pltpu.VMEM((LEN,128),jnp.float32),pltpu.VMEM((LEN,128),jnp.float32)],
        compiler_params=pltpu.CompilerParams(vmem_limit_bytes=48*2**20),
        cost_estimate=cost(5),
        name="attn_bwd")(qkv,qkv,qkv,grad,lse,tvec)


def bucket_of_offset(offset):
    distance = jnp.abs(offset)
    far_bucket = jnp.full(distance.shape, 8, jnp.int32)
    for edge_value in far_edges:
        far_bucket = far_bucket + (distance >= edge_value).astype(jnp.int32)
    near_bucket = jnp.where(distance < 8, distance, far_bucket)
    return near_bucket + jnp.where(offset > 0, 16, 0)


def adam_step(weight, first, second, grad, rate, bias_one, bias_two, average, smooth_decay):
    first_new = MOMENT_DECAY * first + (1.0 - MOMENT_DECAY) * grad
    second_new = SQUARE_DECAY * second + (1.0 - SQUARE_DECAY) * grad * grad
    direction = first_new / bias_one / (jnp.sqrt(second_new / bias_two) + ADAM_FLOOR)
    weight_new = weight - rate * (direction + WEIGHT_DECAY * weight)
    average_new = smooth_decay * average + (1.0 - smooth_decay) * weight_new
    return (weight_new, first_new, second_new, average_new)


def low(values):
    return values.astype(jnp.bfloat16)


def wide(values):
    return values.astype(jnp.float32)


def tie(*values):
    return lax.optimization_barrier(values)


class Grid:
    def __init__(self, seq_count, batch_count):
        if batch_count == 8:
            digits = [4, 2]
        else:
            digits, rest = [], batch_count
            while rest % 4 == 0:
                digits, rest = [4] + digits, rest // 4
            if rest > 1:
                digits = [rest] + digits
        self.sizes = [seq_count // 2, 2] + digits
        self.total = seq_count * batch_count
        self.batch_dims = list(range(2, len(self.sizes)))
        self.swaps = self.sizes[-1] == self.sizes[0]

    def split(self, index):
        out = []
        for size in reversed(self.sizes):
            out.append(index % size)
            index = index // size
        return out[::-1]

    def join(self, coords):
        index = 0
        for size, coord in zip(self.sizes, coords):
            index = index * size + coord
        return index

    def shift(self, values, dim, step, odd_dim=None):
        pairs = []
        for index in range(self.total):
            coords = self.split(index)
            along = dim if odd_dim is None or coords[1] == 0 else odd_dim
            coords[along] = (coords[along] + step) % self.sizes[along]
            pairs.append((index, self.join(coords)))
        return lax.ppermute(values, AXES, pairs)

    def mine(self):
        return self.split(lax.axis_index(AXES))

    def small_stages(self):
        first = [(dim, dim) for dim in self.batch_dims[:-1]]
        x, y = self.batch_dims[-1], 0
        if self.swaps:
            return first + [(x, y), (y, x), (1, 1)]
        return first + [(x, x), (y, y), (1, 1)]

    def small_owner(self):
        stages = self.small_stages()
        rest = jnp.arange(self.total, dtype=jnp.int32)
        steps = []
        for dim, _ in stages:
            steps.append(rest % self.sizes[dim])
            rest = rest // self.sizes[dim]
        mine = self.mine()
        core = (mine[1] + steps[-1]) % 2
        coords = list(mine)
        coords[1] = core
        for (dim, odd_dim), step in zip(stages[:-1], steps[:-1]):
            if dim == odd_dim:
                coords[dim] = (coords[dim] - step) % self.sizes[dim]
            else:
                for this, other in ((dim, 0), (odd_dim, 1)):
                    coords[this] = jnp.where(
                        core == other, (coords[this] - step) % self.sizes[this], coords[this]
                    )
        return self.join(coords)


def absolute(parts, place):
    count = len(parts)
    if count == 2:
        first = place == 0
        return [jnp.where(first, parts[0], parts[1]), jnp.where(first, parts[1], parts[0])]
    return [
        lax.select_n(lax.rem(place - j + count, count), *parts) for j in range(count)
    ]


class Scatter:
    def __init__(self, grid, pieces, order):
        self.grid = grid
        self.plan = list(order)
        self.sent = False
        self.start(pieces)

    def start(self, pieces):
        dim = self.plan[0]
        count = self.grid.sizes[dim]
        axis = max(dim - 1, 0)
        place = self.grid.mine()[dim]
        if count == 2:
            parts = [lax.slice_in_dim(pieces, j, j + 1, axis=axis) for j in range(count)]
            self.parts = absolute(parts, place)
        else:
            self.parts = [
                lax.dynamic_slice_in_dim(pieces, lax.rem(place - j + count, count), 1, axis)
                for j in range(count)
            ]

    def settle(self):
        self.plan.pop(0)
        total = wide(self.parts[0])
        for part in self.parts[1:]:
            total = total + wide(part)
        self.total = low(total) if self.plan else total
        self.sent = False
        if self.plan:
            self.start(self.total)

    def send(self):
        dim = self.plan[0]
        for step in range(1, len(self.parts)):
            self.parts[step] = self.grid.shift(self.parts[step], dim, -step)
        self.sent = True

    def advance(self, *values):
        if self.sent:
            _, *self.parts = tie(values[0], *self.parts)
            self.settle()
        if self.plan:
            count = len(self.parts) - 1
            tied = tie(*values, *self.parts[1:])
            self.parts[1:] = tied[-count:]
            values = tied[:-count]
            self.send()
        return values[0] if len(values) == 1 else values

    def collect(self, value):
        _, *self.parts = tie(value, *self.parts)
        self.settle()
        value, *self.parts = tie(value, *self.parts)
        return value

    def result(self, value):
        if self.sent:
            _, *self.parts = tie(value, *self.parts)
        while self.plan:
            if self.sent:
                self.settle()
            if self.plan:
                self.send()
        return self.total


def exchange(values):
    return lax.all_to_all(values, ("y", "core"), split_axis=0, concat_axis=0, tiled=True)


def pick(near_ref, far_ref):
    step = pl.program_id(0)
    return jnp.where(step < pl.num_programs(0) // 2, near_ref[...], far_ref[...])


def pair_specs(rows, blocks):
    return [
        pl.BlockSpec((rows, QB), lambda t, core: (0, jnp.minimum(t, blocks - 1))),
        pl.BlockSpec((rows, QB), lambda t, core: (0, jnp.maximum(t - blocks, 0))),
    ]


def by_core(kernel, grid, in_specs, out_specs, out_shape, name, micros):
    return pl.pallas_call(
        lambda core_ref, *refs: kernel(*refs),
        grid_spec=pltpu.PrefetchScalarGridSpec(
            num_scalar_prefetch=1, grid=grid, in_specs=in_specs, out_specs=out_specs
        ),
        out_shape=out_shape,
        compiler_params=pltpu.CompilerParams(vmem_limit_bytes=56 * MIB),
        cost_estimate=cost(micros),
        name=name,
    )


def weight_spec(first):
    return pl.BlockSpec((1, FF // 2, D), lambda t, core: (first + core[0], 0, 0))


def token_spec(rows, first=0):
    return pl.BlockSpec((rows, QB), lambda t, core: (0, first + t))


def lift_kernel(near_ref, far_ref, g_ref, u_ref, units_ref, da_ref, db_ref):
    block = pick(near_ref, far_ref)
    rows = units_ref.shape[0] // 2
    for part in range(2):
        here = slice(part * rows, (part + 1) * rows)
        gate = mm(g_ref[0, here, :], block)
        up = mm(u_ref[0, here, :], block)
        root = 0.7978845608028654
        square = gate * gate
        inside = jnp.tanh(root * gate * (1.0 + 0.044715 * square))
        half = 0.5 * (1.0 + inside)
        active = gate * half
        slope = half + 0.5 * gate * (1.0 - inside * inside) * (
            root * (1.0 + 3.0 * 0.044715 * square)
        )
        units_ref[here, :] = low(active * up)
        da_ref[here, :] = low(up * slope)
        db_ref[here, :] = low(active)


def lift(core, near, far, inner_full):
    tokens = 2 * near.shape[1]
    blocks = near.shape[1] // QB
    out = jax.ShapeDtypeStruct((FF // 2, tokens), jnp.bfloat16)
    return by_core(
        lift_kernel,
        (2 * blocks,),
        pair_specs(D, blocks) + [weight_spec(0), weight_spec(2)],
        [token_spec(FF // 2)] * 3,
        [out] * 3,
        "lift",
        5,
    )(core, near, far, inner_full, inner_full)


def unlift_kernel(near_ref, far_ref, w_ref, da_ref, db_ref, out_ref):
    half = w_ref.shape[1]
    units_grad = mm(w_ref[0], pick(near_ref, far_ref))
    out_ref[:half, :] = low(units_grad * wide(da_ref[...]))
    out_ref[half:, :] = low(units_grad * wide(db_ref[...]))


def unlift(core, near, far, outer_full, slope_gate, slope_up):
    tokens = 2 * near.shape[1]
    blocks = near.shape[1] // QB
    return by_core(
        unlift_kernel,
        (2 * blocks,),
        pair_specs(D, blocks) + [weight_spec(0)] + [token_spec(FF // 2)] * 2,
        token_spec(FF),
        jax.ShapeDtypeStruct((FF, tokens), jnp.bfloat16),
        "unlift",
        3,
    )(core, near, far, outer_full, slope_gate, slope_up)


def lower_kernel(w_ref, units_ref, out_ref):
    out_ref[...] = mm(w_ref[0], units_ref[...], TN).astype(out_ref.dtype)


def lower(core, outer_full, units, first, dtype):
    tokens = units.shape[1] // 2
    return by_core(
        lower_kernel,
        (tokens // QB,),
        [weight_spec(0), token_spec(FF // 2, first * (tokens // QB))],
        token_spec(D),
        jax.ShapeDtypeStruct((D, tokens), dtype),
        "lower",
        2,
    )(core, outer_full, units)


def states_grad_kernel(g_ref, u_ref, grad_ref, out_ref):
    half = g_ref.shape[1]
    total = mm(g_ref[0], grad_ref[:half, :], TN)
    out_ref[...] = (total + mm(u_ref[0], grad_ref[half:, :], TN)).astype(out_ref.dtype)


def states_grad(core, inner_full, lifted_grad, first, dtype):
    tokens = lifted_grad.shape[1] // 2
    return by_core(
        states_grad_kernel,
        (tokens // QB,),
        [weight_spec(0), weight_spec(2), token_spec(FF, first * (tokens // QB))],
        token_spec(D),
        jax.ShapeDtypeStruct((D, tokens), dtype),
        "states_grad",
        0,
    )(core, inner_full, inner_full, lifted_grad)


def whole(shape):
    return pl.BlockSpec(shape, lambda *_: (0,) * len(shape))


def weight_grad_kernel(block, half, left_ref, near_ref, far_ref, out_ref):
    tokens = near_ref.shape[1]
    left = left_ref[...]
    if half is not None:
        starts = range(half * (block // 2), left.shape[0], block)
        left = jnp.concatenate([left[start : start + block // 2] for start in starts], axis=0)
    total = mm(left[:, :tokens], near_ref[...], NT)
    out_ref[...] = low(total + mm(left[:, tokens:], far_ref[...], NT))


def weight_grad(left, near, far, count, block=None, half=None):
    tokens = near.shape[1]
    tile = left.shape[0] // count
    rows = tile if half is None else tile // 2
    return pl.pallas_call(
        functools.partial(weight_grad_kernel, block, half),
        grid=(count,),
        in_specs=[
            pl.BlockSpec((tile, 2 * tokens), lambda f: (f, 0)),
            whole((D, tokens)),
            whole((D, tokens)),
        ],
        out_specs=pl.BlockSpec((rows, D), lambda f: (f, 0)),
        out_shape=jax.ShapeDtypeStruct((count * rows, D), jnp.bfloat16),
        compiler_params=pltpu.CompilerParams(vmem_limit_bytes=56 * MIB),
        cost_estimate=cost(2),
        name="weight_grad",
    )(left, near, far)


def scale_of(values):
    return lax.rsqrt(jnp.mean(values * values, axis=0, keepdims=True) + EPSILON)


def add_line(line_ref, values):
    total = jnp.sum(values, axis=1, keepdims=True)

    @pl.when(pl.program_id(0) == 0)
    def _():
        line_ref[...] = total

    @pl.when(pl.program_id(0) > 0)
    def _():
        line_ref[...] += total


def back_through_norm(values, scale, weighted):
    inner_mean = jnp.mean(weighted * values, axis=0, keepdims=True)
    return scale * weighted - values * (scale * scale * scale * inner_mean)


def gate_kernel(
    middle_ref, near_ref, far_ref, state_ref, cot_ref, keep_ref, gain_ref,
    result_ref, grad_ref, low_ref, gate_ref, line_ref,
):
    result = middle_ref[...] + near_ref[...] + wide(far_ref[...])
    result_ref[0] = low(result)
    scale = scale_of(result)
    gain = gain_ref[...]
    dot = jnp.sum(result * gain, axis=0, keepdims=True)
    squashed = jax.nn.sigmoid(dot * scale)
    keep = keep_ref[0]
    gate_ref[0] = GATE_RANGE * squashed * keep
    logit_grad = cot_ref[0] * keep * GATE_RANGE * squashed * (1.0 - squashed)
    share = logit_grad * scale
    grad = (
        wide(state_ref[0]) + share * gain - result * (share * scale * scale * dot * (1.0 / D))
    )
    grad_ref[...] = grad
    low_ref[...] = low(grad)
    add_line(line_ref, share * result)


def mid_kernel(near_ref, far_ref, middle_ref, grad_ref, gain_ref, out_ref, low_ref, line_ref):
    normed_grad = near_ref[...] + wide(far_ref[...])
    middle = middle_ref[...]
    scale = scale_of(middle)
    total = grad_ref[...] + back_through_norm(middle, scale, normed_grad * gain_ref[...])
    out_ref[...] = total
    low_ref[...] = low(total)
    add_line(line_ref, normed_grad * middle * scale)


def last_kernel(w_ref, projected_ref, hidden_ref, grad_ref, gain_ref, out_ref, line_ref):
    normed_grad = mm(w_ref[...], projected_ref[...], (((0,), (1,)), ((), ())))
    hidden = wide(hidden_ref[0])
    scale = scale_of(hidden)
    out_ref[0] = low(
        grad_ref[...] + back_through_norm(hidden, scale, normed_grad * gain_ref[...])
    )
    add_line(line_ref, normed_grad * hidden * scale)


WIDE = pl.BlockSpec((D, QB), lambda t: (0, t))
ROW = pl.BlockSpec((1, D, QB), lambda t: (t, 0, 0))
THIN = pl.BlockSpec((1, 1, QB), lambda t: (t, 0, 0))
COLUMN = pl.BlockSpec((D, 1), lambda t: (0, 0))
COLUMN_SHAPE = jax.ShapeDtypeStruct((D, 1), jnp.float32)


def over_blocks(kernel, count, in_specs, out_specs, out_shape, name):
    return pl.pallas_call(
        kernel,
        grid=(count,),
        in_specs=in_specs,
        out_specs=out_specs,
        out_shape=out_shape,
        compiler_params=pltpu.CompilerParams(vmem_limit_bytes=56 * MIB),
        cost_estimate=cost(0),
        name=name,
    )


def spread_kernel(rank_ref, cot_ref, out_ref):
    slot = lax.broadcasted_iota(jnp.int32, (KEEP_CAP, QB), 0)
    chosen = low(jnp.where(slot == rank_ref[0], 1.0, 0.0))
    out_ref[0] = low(mm(cot_ref[...], chosen))


def spread(rank, cotangent):
    blocks = rank.shape[0]
    return pl.pallas_call(
        spread_kernel,
        grid=(blocks,),
        in_specs=[
            pl.BlockSpec((1, 1, QB), lambda i: (i, 0, 0)),
            pl.BlockSpec((D, KEEP_CAP), lambda i: (0, 0)),
        ],
        out_specs=pl.BlockSpec((1, D, QB), lambda i: (i, 0, 0)),
        out_shape=jax.ShapeDtypeStruct((blocks, D, QB), jnp.bfloat16),
        compiler_params=pltpu.CompilerParams(vmem_limit_bytes=40 * MIB),
        cost_estimate=cost(1),
        name="spread",
    )(rank, cotangent)


def compact_kernel(rank_ref, rows_ref, out_ref, sum_ref):
    slot = lax.broadcasted_iota(jnp.int32, (QB, KEEP_CAP), 1)
    chosen = low(jnp.where(slot == rank_ref[0], 1.0, 0.0))
    part = mm(rows_ref[0], chosen)

    @pl.when(pl.program_id(0) == 0)
    def _():
        sum_ref[...] = part

    @pl.when(pl.program_id(0) > 0)
    def _():
        sum_ref[...] += part

    @pl.when(pl.program_id(0) == pl.num_programs(0) - 1)
    def _():
        out_ref[...] = low(sum_ref[...])


def compact(rank, rows):
    blocks = rank.shape[0]
    return pl.pallas_call(
        compact_kernel,
        grid=(blocks,),
        in_specs=[
            pl.BlockSpec((1, QB, 1), lambda i: (i, 0, 0)),
            pl.BlockSpec((1, D, QB), lambda i: (i, 0, 0)),
        ],
        out_specs=pl.BlockSpec((D, KEEP_CAP), lambda i: (0, 0)),
        out_shape=jax.ShapeDtypeStruct((D, KEEP_CAP), jnp.bfloat16),
        scratch_shapes=[pltpu.VMEM((D, KEEP_CAP), jnp.float32)],
        compiler_params=pltpu.CompilerParams(vmem_limit_bytes=40 * MIB),
        cost_estimate=cost(1),
        name="compact",
    )(rank, rows)


def per_device(
    seq_count,
    batch_count,
    hidden,
    keep_mask,
    states_cotangent,
    gate_cotangent,
    step_count,
    attend_weight,
    attend_first,
    attend_second,
    attend_average,
    output_weight,
    output_first,
    output_second,
    output_average,
    inner_weight,
    inner_first,
    inner_second,
    inner_average,
    outer_weight,
    outer_first,
    outer_second,
    outer_average,
    norm_params,
    norm_first,
    norm_second,
    norm_average,
    bias_table,
    table_first,
    table_second,
    table_average,
):
    grid = Grid(seq_count, batch_count)
    batch_dims = grid.batch_dims
    batch_sizes = [grid.sizes[dim] for dim in batch_dims]
    ones = (1,) * len(batch_dims)
    seq_place = lax.axis_index(("y", "core"))
    row_count, shard_len = hidden.shape[0], hidden.shape[1]
    tokens = row_count * shard_len
    attend_rows, output_rows = attend_weight.shape[1], output_weight.shape[0]
    inner_rows, outer_rows = inner_weight.shape[1], outer_weight.shape[0]
    half_ff = FF // 2

    core = lax.axis_index("core").reshape(1).astype(jnp.int32)
    small_rows = attend_rows + output_rows
    small = jnp.concatenate([low(attend_weight).T, low(output_weight)], axis=0)[None]
    stages = grid.small_stages()

    def small_stage(blocks, stage):
        dim, odd_dim = stage
        parts = [blocks] + [
            grid.shift(blocks, dim, step, odd_dim) for step in range(1, grid.sizes[dim])
        ]
        return jnp.concatenate(parts, axis=0)

    swapped = []
    for index in range(grid.total):
        y, core_place, *rest = grid.split(index)
        swapped.append((index, grid.join([core_place, y] + rest)))
    small = small_stage(small, stages[0])
    inner_piece = low(inner_weight).T
    hidden, inner_piece = tie(hidden, inner_piece)
    owner = grid.small_owner()[:, None]

    def choose_rows(rows, width):
        ids = (owner * rows + jnp.arange(rows, dtype=jnp.int32)[None, :]).reshape(1, -1)
        return low(jnp.arange(width, dtype=jnp.int32)[:, None] == ids)

    ids = jnp.arange(small_rows, dtype=jnp.int32)[None, :]
    place = jnp.where(
        ids < attend_rows,
        owner * attend_rows + ids,
        3 * INNER + owner * output_rows + ids - attend_rows,
    ).reshape(1, -1)
    choose = low(jnp.arange(4 * INNER, dtype=jnp.int32)[:, None] == place)
    choose_attend = choose_rows(attend_rows, 3 * INNER)
    choose_output = choose_rows(output_rows, INNER)
    choose_attend, choose_output = tie(choose_attend, choose_output)

    back_orders = [batch_dims[:0:-1] + [0] + batch_dims[:1], [0] + batch_dims[::-1]]

    def by_token(values):
        return values.transpose(1, 0, 2).reshape(D, tokens)

    def to_rows(values):
        width = values.shape[-1]
        return exchange(values.reshape(row_count, shard_len, width)).reshape(LEN, width)

    def to_positions(values):
        width = values.shape[-1]
        return exchange(values.reshape(seq_count, shard_len, width)).reshape(tokens, width)

    own_keep = lax.dynamic_slice_in_dim(keep_mask, seq_place, 1, 0)
    own_rank = jnp.where(own_keep > 0, jnp.cumsum(own_keep, axis=1) - 1, -1)
    own_rank = own_rank.reshape(LEN // QB, QB)

    hidden_in = wide(by_token(hidden.transpose(0, 2, 1)))

    gains = norm_params[:, :, None]
    scale_one = scale_of(hidden_in)
    normed_one = low(hidden_in * scale_one * gains[0])
    cotangents = spread(own_rank[:, None, :], states_cotangent.reshape(KEEP_CAP, D).T)
    small, normed_one = tie(small, normed_one)
    for stage in stages[1:-1]:
        small = small_stage(small, stage)
    small, inner_piece = tie(small, inner_piece)
    inner_full = lax.all_gather(inner_piece, AXES, axis=0, tiled=True)
    inner_full = inner_full.reshape(4, FF // 2, D)
    _, outer_piece = tie(small, low(outer_weight))
    outer_full = lax.all_gather(outer_piece, AXES, axis=0, tiled=True)
    outer_full = outer_full.reshape(2, FF // 2, D)
    small = small_stage(small, stages[-1]).reshape(grid.total * small_rows, D)
    attend_full = low(mm(choose[: 3 * INNER], small))
    projected = low(mm(normed_one, attend_full, (((0,), (1,)), ((), ()))))
    _, small = tie(projected, small)
    output_full = low(mm(choose[3 * INNER :], small))
    row_projected = to_rows(projected)
    window = jnp.arange(WB, dtype=jnp.int32)
    offsets = jnp.where(window >= WB - QB, window - WB, window) - (LEN - QB)
    one_hot = wide(
        bucket_of_offset(offsets)[:, None] == jnp.arange(BUCKETS, dtype=jnp.int32)[None, :]
    )
    bias_line = jnp.sum(bias_table[:, None, :] * one_hot[None], axis=-1)
    bias_line = bias_line.reshape(HEADS // 2, 2, WB)
    row_projected, output_full = tie(row_projected, output_full)
    row_mixed, row_lse = attn_fwd(row_projected, bias_line)
    mixed = to_positions(row_mixed)
    mixed, cotangents = tie(mixed, cotangents)
    cotangents, row_mixed = tie(cotangents, row_mixed)
    mixed, cotangents = tie(mixed, cotangents)
    middle = hidden_in + mm(output_full, mixed, (((0,), (1,)), ((), ())))
    scale_two = scale_of(middle)
    normed_two = low(middle * scale_two * gains[1])
    far_states = grid.shift(normed_two, 1, 1)

    _, inner_full = tie(normed_two, inner_full)
    inner_full, cotangents = tie(inner_full, cotangents)
    cotangents = exchange(cotangents)
    units, slope_gate, slope_up = lift(core, normed_two, far_states, inner_full)
    _, outer_full = tie(units, outer_full)
    far_part = lower(core, outer_full, units, 1, jnp.bfloat16)
    units, far_part, cotangents = tie(units, far_part, cotangents)
    near_part = lower(core, outer_full, units, 0, jnp.float32)

    blocks = tokens // QB
    keep_local = lax.dynamic_slice_in_dim(keep_mask, seq_place * shard_len, shard_len, 1)
    wide_shape = jax.ShapeDtypeStruct((D, tokens), jnp.float32)
    low_shape = jax.ShapeDtypeStruct((D, tokens), jnp.bfloat16)
    row_shape = jax.ShapeDtypeStruct((blocks, D, QB), jnp.bfloat16)
    thin_shape = jax.ShapeDtypeStruct((blocks, 1, QB), jnp.float32)
    row_result, result_grad, result_grad_low, kept_gate, line_grad = over_blocks(
        gate_kernel,
        blocks,
        [WIDE, WIDE, WIDE, ROW, THIN, THIN, COLUMN],
        [ROW, WIDE, WIDE, THIN, COLUMN],
        [row_shape, wide_shape, low_shape, thin_shape, COLUMN_SHAPE],
        "gate",
    )(
        middle,
        near_part,
        grid.shift(far_part, 1, 1),
        cotangents,
        gate_cotangent.reshape(blocks, 1, QB),
        wide(keep_local).reshape(blocks, 1, QB),
        gains[2] * gains[3],
    )
    kept_gate = kept_gate.reshape(row_count, shard_len)
    line_grad = line_grad[:, 0]
    row_result = exchange(row_result)
    far_grads = grid.shift(result_grad_low, 1, 1)

    lifted_grad = unlift(core, result_grad_low, far_grads, outer_full, slope_gate, slope_up)
    scatters = []
    for h in range(2):
        if inner_rows % 32 == 0:
            grad = weight_grad(lifted_grad, normed_two, far_states, 4, inner_rows, h)
        else:
            grad = weight_grad(lifted_grad, normed_two, far_states, 8)
            grad = grad.reshape(-1, 2, inner_rows // 2, D)[:, h]
        grad = grad.reshape([2] + batch_sizes + [inner_rows // 2, D])
        scatters.append(Scatter(grid, grad, back_orders[h]))
        lifted_grad = scatters[h].advance(lifted_grad)
    far_part = states_grad(core, inner_full, lifted_grad, 1, jnp.bfloat16)
    lifted_grad, far_part, row_result = tie(lifted_grad, far_part, row_result)
    far_part = grid.shift(far_part, 1, 1)
    near_part = states_grad(core, inner_full, lifted_grad, 0, jnp.float32)
    near_part = scatters[0].collect(near_part)
    middle_grad, middle_grad_low, feed_line = over_blocks(
        mid_kernel,
        blocks,
        [WIDE, WIDE, WIDE, WIDE, COLUMN],
        [WIDE, WIDE, COLUMN],
        [wide_shape, low_shape, COLUMN_SHAPE],
        "mid",
    )(near_part, far_part, middle, result_grad, gains[1])
    feed_line = feed_line[:, 0]

    mixed_grad = low(mm(middle_grad_low, output_full, (((0,), (1,)), ((), ()))))
    units, mixed_grad = tie(units, mixed_grad)
    row_mixed_grad = to_rows(mixed_grad)
    outer_grad = weight_grad(units, result_grad_low, far_grads, 4)
    chosen_mixed = low(mm(mixed, choose_output))
    output_grad = low(mm(chosen_mixed, middle_grad_low, (((0,), (1,)), ((), ()))))
    row_mixed_grad, output_grad, outer_grad = tie(row_mixed_grad, output_grad, outer_grad)
    outer_sum = lax.psum_scatter(outer_grad, ("y", "batch"), scatter_dimension=0, tiled=True)
    row_mixed_grad = scatters[0].advance(row_mixed_grad)
    row_mixed_grad = scatters[1].advance(row_mixed_grad)
    row_grad, line_sums = attn_bwd(row_projected, row_mixed_grad, row_lse, bias_line)
    row_grad = scatters[0].advance(row_grad)
    row_grad = scatters[1].advance(row_grad)
    projected_grad = to_positions(row_grad)
    kept_states = compact(own_rank[:, :, None], row_result).T.reshape(1, 1, KEEP_CAP, D)
    one_hot_rows = jnp.stack([jnp.roll(one_hot, r, axis=0) for r in range(8)])
    table_grad = jnp.einsum(
        "hrw,rwb->hb",
        line_sums.reshape(HEADS, 8, WB),
        one_hot_rows,
        precision=lax.Precision.HIGHEST,
    )
    inner_sum0 = scatters[0].result(table_grad).reshape(inner_rows // 2, D)
    inner_sum1 = scatters[1].result(table_grad).reshape(inner_rows // 2, D)
    projected_grad, kept_states, table_grad, inner_sum0, inner_sum1 = tie(
        projected_grad, kept_states, table_grad, inner_sum0, inner_sum1
    )
    chosen_grad = low(mm(projected_grad, choose_attend))

    def swap(values, bit):
        pairs = [(index, index ^ bit) for index in range(grid.total)]
        return lax.ppermute(values, AXES, pairs)

    small_grads = [
        low(mm(chosen_grad, normed_one, (((0,), (1,)), ((), ())))),
        output_grad,
    ]
    bits = [1 << place for place in range((grid.total - 1).bit_length())]
    for index, (dim, odd_dim) in enumerate(stages[::-1]):
        count = grid.sizes[dim]
        parts = [jnp.split(grad, count, axis=0) for grad in small_grads]
        totals = [wide(part[0]) for part in parts]
        sends = [
            jnp.concatenate([part[step] for part in parts], axis=0) for step in range(1, count)
        ]
        if index > 0:
            if index == 2:
                outer_sum, *sends = tie(outer_sum, *sends)
            lines, *sends = tie(lines, *sends)
            lines = lines + swap(lines, bits.pop(0))
        moved = [grid.shift(send, dim, -step - 1, odd_dim) for step, send in enumerate(sends)]
        if index == 0:
            input_grad, attend_line = over_blocks(
                last_kernel,
                blocks,
                [
                    whole((3 * INNER, D)),
                    pl.BlockSpec((QB, 3 * INNER), lambda t: (t, 0)),
                    ROW,
                    WIDE,
                    COLUMN,
                ],
                [ROW, COLUMN],
                [row_shape, COLUMN_SHAPE],
                "last",
            )(attend_full, projected_grad, hidden.transpose(0, 2, 1), middle_grad, gains[0])
            attend_line = attend_line[:, 0]
            lines = jnp.stack(
                [
                    attend_line,
                    feed_line,
                    line_grad * norm_params[3],
                    line_grad * norm_params[2],
                    jnp.pad(table_grad.reshape(-1), (0, D - HEADS * BUCKETS)),
                ]
            )
        rows = totals[0].shape[0]
        for part in moved:
            totals = [totals[0] + wide(part[:rows]), totals[1] + wide(part[rows:])]
        small_grads = [low(total) for total in totals]
    while bits:
        lines = lines + swap(lines, bits.pop(0))
    input_grad = input_grad.transpose(0, 2, 1)

    inner_sum = jnp.concatenate([inner_sum0, inner_sum1], axis=0).T
    outer_sum = wide(lax.ppermute(outer_sum, AXES, swapped))
    attend_sum = totals[0].T
    output_sum = totals[1]
    norm_total = lines[:4]
    table_total = lines[4, : HEADS * BUCKETS].reshape(HEADS, BUCKETS)

    steps_done = wide(step_count[0])
    bias_one = 1.0 - MOMENT_DECAY**steps_done
    bias_two = 1.0 - SQUARE_DECAY**steps_done
    smooth_decay = (1.0 + steps_done) / (10.0 + steps_done)

    def updated(weight, first, second, grad, rate, average):
        return adam_step(
            weight, first, second, grad, rate, bias_one, bias_two, average, smooth_decay
        )

    return (
        kept_states,
        kept_gate,
        input_grad,
        *updated(
            attend_weight, attend_first, attend_second, attend_sum, RATE_ATTEND, attend_average
        ),
        *updated(
            output_weight, output_first, output_second, output_sum, RATE_OUTPUT, output_average
        ),
        *updated(inner_weight, inner_first, inner_second, inner_sum, RATE_INNER, inner_average),
        *updated(outer_weight, outer_first, outer_second, outer_sum, RATE_OUTER, outer_average),
        *updated(norm_params, norm_first, norm_second, norm_total, RATE_NORM, norm_average),
        *updated(bias_table, table_first, table_second, table_total, RATE_TABLE, table_average),
    )


def solution(mesh):
    placed = (
        P("batch", ("y", "core"), None),
        P("batch", None),
        P("batch", ("y", "core"), None, None),
        P("batch", ("y", "core")),
        P(),
        P(None, ("y", "core", "batch")),
        P(None, ("y", "core", "batch")),
        P(None, ("y", "core", "batch")),
        P(None, ("y", "core", "batch")),
        P(("y", "core", "batch"), None),
        P(("y", "core", "batch"), None),
        P(("y", "core", "batch"), None),
        P(("y", "core", "batch"), None),
        P(None, ("y", "core", "batch")),
        P(None, ("y", "core", "batch")),
        P(None, ("y", "core", "batch")),
        P(None, ("y", "core", "batch")),
        P(("y", "core", "batch"), None),
        P(("y", "core", "batch"), None),
        P(("y", "core", "batch"), None),
        P(("y", "core", "batch"), None),
        P(),
        P(),
        P(),
        P(),
        P(),
        P(),
        P(),
        P(),
    )
    devices = mesh.devices.reshape(mesh.shape["seq"] // 2, 2, mesh.shape["batch"])
    finer = jax.sharding.Mesh(devices, ("y", "core", "batch"))
    return jax.shard_map(
        functools.partial(per_device, mesh.shape["seq"], mesh.shape["batch"]),
        mesh=finer,
        in_specs=placed,
        out_specs=(
            P("batch", ("y", "core"), None, None),
            P("batch", ("y", "core")),
            P("batch", ("y", "core"), None),
            P(None, ("y", "core", "batch")),
            P(None, ("y", "core", "batch")),
            P(None, ("y", "core", "batch")),
            P(None, ("y", "core", "batch")),
            P(("y", "core", "batch"), None),
            P(("y", "core", "batch"), None),
            P(("y", "core", "batch"), None),
            P(("y", "core", "batch"), None),
            P(None, ("y", "core", "batch")),
            P(None, ("y", "core", "batch")),
            P(None, ("y", "core", "batch")),
            P(None, ("y", "core", "batch")),
            P(("y", "core", "batch"), None),
            P(("y", "core", "batch"), None),
            P(("y", "core", "batch"), None),
            P(("y", "core", "batch"), None),
            P(),
            P(),
            P(),
            P(),
            P(),
            P(),
            P(),
            P(),
        ),
        check_vma=False,
    )
```
